128 devices in a mesh: tm: 16 (over x, y), space: 8 (over z, core).
Axes of the slice: x: 4, y: 4, z: 4, core: 2. Of those that a mesh axis runs over, the one named last changes fastest.
Arguments:
- frames: bfloat16 [8192, 8, 256], P('tm', 'space'), may hold values from -8 to 8
- patch_cell: int32 [8], P('space'), may hold values from 0 to 2047
- enc_in: bfloat16 [256, 1024], replicated, may hold values from -0.375 to 0.375
- enc_bias: float32 [1024], replicated, may hold values from -3 to 3
- enc_out: bfloat16 [1024, 1024], replicated, may hold values from -0.1875 to 0.1875
- pos_table: bfloat16 [2048, 1024], replicated, may hold values from -3 to 3
- norm_gain: float32 [1024], replicated, may hold values from 0.1 to 1.9
- w_pair: bfloat16 [1024, 4096], replicated, may hold values from -0.1875 to 0.1875
- w_keys: bfloat16 [1024, 256], replicated, may hold values from -0.0234375 to 0.0234375
- w_step: bfloat16 [1024, 32], replicated, may hold values from -0.1875 to 0.1875
- step_bias: float32 [32], replicated, may hold values from -1.5 to 1
- decay_code: int32 [32], replicated, may hold values from 0 to 15
- skip_gain: float32 [32], replicated, may hold values from 0.5 to 1.5
- out_gain: float32 [2048], replicated, may hold values from 0.1 to 1.9
- w_out: bfloat16 [2048, 1024], replicated, may hold values from -0.125 to 0.125
Outputs:
- layer_output: bfloat16 [8192, 8, 1024], P('tm', 'space')
The draws below stay inside these ranges and needn't reach their ends.
All inputs are finite; a program needn't handle non-finite values.
Results may differ from the reference program's by a relative error of at most 0.013.
Values may be sent and summed in bfloat16 or wider, within the bound.
A program may use at most 128 MiB of HBM per device.

```python
import jax
import jax.numpy as jnp
from jax import lax

D = 1024
PIX = 256
HEADS = 32
HD = 64
N = 128
GRID = 2048
TB = 512
TIME = 8192
PATCHES = 8
N_TM = 16


def draw_frames(key, part):
    key_noise = jax.random.fold_in(key, 11)
    key_level = jax.random.fold_in(key, 12)
    key_shape = jax.random.fold_in(key, 13)
    noise = jnp.clip(jax.random.normal(key_noise, (TIME, PATCHES, PIX), jnp.float32), -5.0, 5.0)
    run_len = TB // 4
    levels = jax.random.uniform(key_level, (TIME // run_len,), jnp.float32, -2.0, 2.0)
    level_rows = jnp.repeat(levels, run_len)
    pattern = jnp.clip(0.7 * jax.random.normal(key_shape, (PATCHES, PIX), jnp.float32), -2.0, 2.0)
    values = noise + level_rows[:, None, None] * pattern[None]
    return jnp.clip(values, -8.0, 8.0).astype(jnp.bfloat16)


def plant(values, own_key, low, high):
    longest = values.shape.index(max(values.shape))
    spots = []
    for shift in (0, 1):
        where = [jax.random.randint(jax.random.fold_in(own_key, axis), (), 0, length) for axis, length in enumerate(values.shape)]
        where[longest] = (where[longest] + shift) % values.shape[longest]
        spots.append(tuple(where))
    return values.at[spots[0]].set(low).at[spots[1]].set(high)


def scatter_about(stream_key, dims, scale, most, kind=jnp.bfloat16):
    drawn = jax.random.normal(stream_key, dims, jnp.float32) * scale
    return jnp.minimum(jnp.maximum(drawn, -most), most).astype(kind)


def setup_inputs(seed: int = 0) -> dict:
    seeds = jax.random.split(jax.random.key(seed), 16)
    frames = draw_frames(jax.random.fold_in(seeds[15], 71), 0)
    patch_cell = plant(jax.random.randint(seeds[1], (PATCHES,), 0, GRID), jax.random.fold_in(seeds[1], 1), 0, GRID - 1).astype(jnp.int32)
    enc_in = scatter_about(seeds[2], (PIX, D), PIX ** -0.5, 0.375)
    enc_bias = scatter_about(seeds[3], (D,), 0.5, 3.0, jnp.float32)
    enc_out = scatter_about(seeds[4], (D, D), D ** -0.5, 0.1875)
    pos_table = scatter_about(seeds[5], (GRID, D), 0.5, 3.0)
    norm_gain = jnp.clip(1.0 + 0.18 * jax.random.normal(seeds[6], (D,), jnp.float32), 0.1, 1.9)
    w_pair = scatter_about(seeds[7], (D, HEADS * 2 * HD), D ** -0.5, 0.1875)
    w_keys = scatter_about(seeds[8], (D, 2 * N), (64 * D) ** -0.5, 0.0234375)
    w_step = scatter_about(seeds[9], (D, HEADS), D ** -0.5, 0.1875)
    step_bias = jnp.clip(jax.random.uniform(seeds[10], (HEADS,), jnp.float32, -1.5, 1.0), -1.5, 1.0)
    decay_code = plant(jax.random.randint(seeds[11], (HEADS,), 0, 16), jax.random.fold_in(seeds[11], 1), 0, 15).astype(jnp.int32)
    skip_gain = jnp.clip(jax.random.uniform(seeds[12], (HEADS,), jnp.float32, 0.5, 1.5), 0.5, 1.5)
    out_gain = jnp.clip(1.0 + 0.18 * jax.random.normal(seeds[13], (HEADS * HD,), jnp.float32), 0.1, 1.9)
    w_out = scatter_about(seeds[14], (HEADS * HD, D), (HEADS * HD) ** -0.5, 0.125)
    return dict(frames=frames, patch_cell=patch_cell, enc_in=enc_in, enc_bias=enc_bias, enc_out=enc_out, pos_table=pos_table, norm_gain=norm_gain, w_pair=w_pair, w_keys=w_keys, w_step=w_step, step_bias=step_bias, decay_code=decay_code, skip_gain=skip_gain, out_gain=out_gain, w_out=w_out)


def rate_table(decay_code):
    return -0.0005 - 0.003 * decay_code.astype(jnp.float32)

def encode(frame_block, pos_rows, enc_in, enc_bias, enc_out, norm_gain):
    hidden = jax.nn.gelu(jnp.dot(frame_block, enc_in, preferred_element_type=jnp.float32) + enc_bias, approximate=True).astype(jnp.bfloat16)
    encoded = (jnp.dot(hidden, enc_out, preferred_element_type=jnp.float32) + pos_rows.astype(jnp.float32)).astype(jnp.bfloat16)
    widened = encoded.astype(jnp.float32)
    normed = (widened * lax.rsqrt(lax.optimization_barrier(jnp.mean(widened * widened, axis=-1, keepdims=True)) + 1e-05) * norm_gain).astype(jnp.bfloat16)
    return (encoded, normed)

def patch_scan(x_vals, z_vals, step_sizes, key_rows, rate_row, skip_row, gain_rows, state_in):
    width = key_rows.shape[-1] // 2
    b_rows = key_rows[:, :width]
    c_rows = key_rows[:, width:]
    cumlog = jnp.cumsum(step_sizes.astype(jnp.float32) * rate_row[None, :], axis=0)
    scores = jnp.dot(c_rows, b_rows.T, preferred_element_type=jnp.float32)
    length = x_vals.shape[0]
    causal = lax.broadcasted_iota(jnp.int32, (length, length), 0) >= lax.broadcasted_iota(jnp.int32, (length, length), 1)
    log_gap = cumlog.T[:, :, None] - cumlog.T[:, None, :]
    weights = (jnp.where(causal[None], jnp.exp(jnp.where(causal[None], log_gap, 0.0)), 0.0) * scores[None]).astype(jnp.bfloat16)
    inner_part = jnp.einsum('hts,shd->thd', weights.astype(jnp.float32), x_vals.astype(jnp.float32))
    to_end = jnp.exp(cumlog[-1][None, :] - cumlog)
    decayed_keys = (to_end[:, :, None] * b_rows.astype(jnp.float32)[:, None, :]).astype(jnp.bfloat16)
    block_state = jnp.einsum('shn,shd->hnd', decayed_keys.astype(jnp.float32), x_vals.astype(jnp.float32))
    carried = jnp.exp(cumlog)[:, :, None] * jnp.einsum('tn,hnd->thd', c_rows.astype(jnp.float32), state_in, precision=lax.Precision.HIGHEST)
    summed = inner_part + carried + skip_row[None, :, None] * x_vals.astype(jnp.float32)
    gated = summed * jax.nn.silu(z_vals.astype(jnp.float32))
    normed = gated * lax.rsqrt(lax.optimization_barrier(jnp.mean(gated * gated, axis=-1, keepdims=True)) + 1e-05) * gain_rows[None]
    new_state = jnp.exp(cumlog[-1])[:, None, None] * state_in + block_state
    return (normed.astype(jnp.bfloat16).reshape(length, -1), new_state)

def reference(frames, patch_cell, enc_in, enc_bias, enc_out, pos_table, norm_gain, w_pair, w_keys, w_step, step_bias, decay_code, skip_gain, out_gain, w_out):
    decay_rates = rate_table(decay_code)
    pos_rows = jnp.take(pos_table, patch_cell, axis=0)
    gain_rows = out_gain.reshape(HEADS, HD)
    split_frames = frames.reshape(N_TM, TB, PATCHES, PIX)

    def one_block(states, frame_block):
        encoded, normed = encode(frame_block, pos_rows, enc_in, enc_bias, enc_out, norm_gain)
        pair_cols = jnp.dot(normed, w_pair, preferred_element_type=jnp.float32).astype(jnp.bfloat16).reshape(TB, PATCHES, HEADS, 2 * HD)
        key_rows = jnp.dot(normed, w_keys, preferred_element_type=jnp.float32).astype(jnp.bfloat16)
        step_sizes = jax.nn.sigmoid(jnp.dot(normed, w_step, preferred_element_type=jnp.float32) + step_bias).astype(jnp.bfloat16)

        def per_patch(packed):
            patch_id, state_in = packed
            pair_one = lax.dynamic_index_in_dim(pair_cols, patch_id, 1, keepdims=False)
            step_one = lax.dynamic_index_in_dim(step_sizes, patch_id, 1, keepdims=False)
            key_one = lax.dynamic_index_in_dim(key_rows, patch_id, 1, keepdims=False)
            return patch_scan(pair_one[..., :HD], pair_one[..., HD:], step_one, key_one, decay_rates, skip_gain, gain_rows, state_in)
        outputs, new_states = lax.map(per_patch, (jnp.arange(PATCHES, dtype=jnp.int32), states))
        merged = jnp.dot(jnp.swapaxes(outputs, 0, 1), w_out, preferred_element_type=jnp.float32)
        return (new_states, (encoded.astype(jnp.float32) + merged).astype(jnp.bfloat16))
    _, result_rows = lax.scan(one_block, jnp.zeros((PATCHES, HEADS, N, HD), jnp.float32), split_frames)
    return result_rows.reshape(TIME, PATCHES, D)
```

```python
import jax
import jax.numpy as jnp
from jax import lax
from jax.sharding import PartitionSpec as P

F32 = jnp.float32
BF16 = jnp.bfloat16


def dot(a, b):
    return jnp.dot(a, b, preferred_element_type=F32)


def body(frames, patch_cell, enc_in, enc_bias, enc_out, pos_table, norm_gain, w_pair, w_keys,
         w_step, step_bias, decay_code, skip_gain, out_gain, w_out):
    count = frames.shape[0]
    heads = w_step.shape[1]
    hd = w_pair.shape[1] // (2 * heads)
    width = w_keys.shape[1] // 2
    peers = lax.axis_size("tm")
    here = lax.axis_index("tm")
    pos_row = lax.dynamic_slice_in_dim(pos_table, patch_cell[0], 1, 0)
    hidden = jax.nn.gelu(dot(frames[:, 0], enc_in) + enc_bias, approximate=True).astype(BF16)
    encoded = (dot(hidden, enc_out) + pos_row.astype(F32)).astype(BF16)
    wide = encoded.astype(F32)
    normed = (
        wide * lax.rsqrt(jnp.mean(wide * wide, axis=-1, keepdims=True) + 1e-05) * norm_gain
    ).astype(BF16)
    pair = dot(normed, w_pair).astype(BF16).reshape(count, heads, 2, hd)
    x = pair[:, :, 0]
    gate = pair[:, :, 1]
    keys = dot(normed, w_keys).astype(BF16)
    b, c = keys[:, :width], keys[:, width:]
    step = jax.nn.sigmoid(dot(normed, w_step) + step_bias).astype(BF16)
    rate = -0.0005 - 0.003 * decay_code.astype(F32)
    causal = lax.broadcasted_iota(jnp.int32, (count, count), 0) >= lax.broadcasted_iota(
        jnp.int32, (count, count), 1
    )
    cum = dot(causal.astype(BF16), step) * rate
    scores = jnp.where(causal, dot(c, b.T), 0.0).astype(BF16)
    scaled = (x.astype(F32) * jnp.exp(-cum)[:, :, None]).astype(BF16).reshape(count, heads * hd)
    total = jnp.exp(cum[-1])
    state = dot(b.T, scaled) * jnp.repeat(total, hd)[None]
    per = heads // peers * hd
    spread = jnp.repeat(total, hd)
    high = spread.astype(BF16)
    low = (spread - high.astype(F32)).astype(BF16)
    outgoing = jnp.concatenate(
        [state.astype(BF16), jnp.broadcast_to(high, (8, heads * hd)),
         jnp.broadcast_to(low, (8, heads * hd))], axis=0
    ).reshape(width + 16, peers, per).swapaxes(0, 1)
    arrived = lax.all_to_all(outgoing, "tm", split_axis=0, concat_axis=0, tiled=True)
    decay = arrived[:, width].astype(F32) + arrived[:, width + 8].astype(F32)
    running = jnp.zeros((width, per), F32)
    entering = []
    for k in range(peers):
        entering.append(running.astype(BF16))
        running = decay[k][None] * running + arrived[k, :width].astype(F32)
    back = lax.all_to_all(jnp.stack(entering), "tm", split_axis=0, concat_axis=0, tiled=True)
    state_in = back.swapaxes(0, 1).reshape(width, heads * hd)
    linear = dot(scores, scaled) + dot(c, state_in)
    y = linear.reshape(count, heads, hd) * jnp.exp(cum)[:, :, None] + skip_gain[None, :, None] * x.astype(F32)
    g = y * jax.nn.silu(gate.astype(F32))
    mixed = (
        g * lax.rsqrt(jnp.mean(g * g, axis=-1, keepdims=True) + 1e-05)
        * out_gain.reshape(heads, hd)[None]
    ).astype(BF16).reshape(count, heads * hd)
    return (encoded.astype(F32) + dot(mixed, w_out)).astype(BF16)[:, None]


def solution(mesh):
    placed = (P("tm", "space", None), P("space")) + (P(),) * 13
    return jax.shard_map(
        body, mesh=mesh, in_specs=placed, out_specs=P("tm", "space", None), check_vma=False
    )
```

```python
import functools

import jax
import jax.numpy as jnp
from jax import lax
from jax.experimental import pallas as pl
from jax.experimental.pallas import tpu as pltpu
from jax.sharding import PartitionSpec as P

F32 = jnp.float32
BF16 = jnp.bfloat16
MESH = pl.DeviceIdType.MESH
GROUPS = 2
LANES = 256
PEERS = 16


def dot(a, b):
    return jnp.dot(a, b, preferred_element_type=F32)


def iota(shape, axis):
    return lax.broadcasted_iota(jnp.int32, shape, axis)


def kernel(
    frames_hbm, enc_in_hbm, enc_out_hbm, w_keys_hbm, w_step_hbm, w_pair_hbm, w_out_hbm,
    pos_ref, enc_bias_ref, norm_gain_ref, step_bias_ref, code_ref, skip_ref, out_gain_ref,
    out_hbm,
    frames, enc_in, enc_out, w_keys, w_step, w_pair, w_out,
    encoded, normed, b_t, c_rows, dec, masked, x_v, xs_v, sz_v, grow_v, y_v, acc, mixed, out_v, skip_lanes,
    end_out, end_in, s_out, s_in, e_out, e_in,
    load_sem, store_sem, end_send, end_recv, send1, recv1, send2, recv2,
):
    count, depth = encoded.shape
    heads = step_bias_ref.shape[1]
    width = c_rows.shape[1]
    lanes_all = x_v.shape[1]
    chunks = lanes_all // LANES
    per = chunks // GROUPS
    hd = lanes_all // heads
    me = lax.axis_index("tm")

    plan = [
        (frames_hbm, frames), (enc_in_hbm, enc_in), (enc_out_hbm, enc_out),
        (w_keys_hbm, w_keys), (w_step_hbm, w_step),
    ]
    loads = [
        pltpu.make_async_copy(src, dst, load_sem.at[n]) for n, (src, dst) in enumerate(plan)
    ]
    half = w_pair.shape[1] // GROUPS
    for g in range(GROUPS):
        loads.append(pltpu.make_async_copy(
            w_pair_hbm.at[:, pl.ds(g * half, half)], w_pair.at[:, pl.ds(g * half, half)],
            load_sem.at[5 + g],
        ))
    loads.append(pltpu.make_async_copy(w_out_hbm, w_out, load_sem.at[5 + GROUPS]))
    for load in loads:
        load.start()

    barrier = pltpu.get_barrier_semaphore()

    def greet(d, carry):
        pl.semaphore_signal(
            barrier, inc=1, device_id={"tm": lax.rem(me + d, PEERS)}, device_id_type=MESH
        )
        return carry

    lax.fori_loop(1, PEERS, greet, 0)

    for n in range(3):
        loads[n].wait()
    rows = 256

    def encode(r, carry):
        at = pl.ds(pl.multiple_of(r * rows, rows), rows)
        hidden = jax.nn.gelu(dot(frames[at, :], enc_in[...]) + enc_bias_ref[...], approximate=True)
        coded = (dot(hidden.astype(BF16), enc_out[...]) + pos_ref[...].astype(F32)).astype(BF16)
        encoded[at, :] = coded
        wide = coded.astype(F32)
        mean = jnp.mean(wide * wide, axis=-1, keepdims=True)
        normed[at, :] = (wide * lax.rsqrt(mean + 1e-05) * norm_gain_ref[...]).astype(BF16)
        return carry

    lax.fori_loop(0, count // rows, encode, 0)

    loads[3].wait()
    loads[4].wait()
    keys = dot(normed[...], w_keys[...]).astype(BF16)
    b_t[...] = keys[:, :width].T
    c_rows[...] = keys[:, width:]
    step = jax.nn.sigmoid(dot(normed[...], w_step[...]) + step_bias_ref[...]).astype(BF16)
    four = (iota((heads, 128), 1) % heads == iota((heads, 128), 0)).astype(BF16)
    step4 = dot(step, four).astype(BF16)
    code4 = dot(jnp.broadcast_to(code_ref[...], (8, heads)).astype(BF16), four)[:1]
    rate4 = -0.0005 - 0.003 * code4
    causal = iota((count, count), 0) >= iota((count, count), 1)
    cum = dot(causal.astype(BF16), step4) * rate4
    lane = iota((count, 128), 1)
    grown = jnp.exp(jnp.where(lane < 2 * heads, cum, -cum))
    high = grown.astype(BF16)
    low = (grown - high.astype(F32)).astype(BF16)
    dec[...] = jnp.where((lane // heads) % 2 == 0, high.astype(F32), low.astype(F32)).astype(BF16)
    end_out[...] = jnp.broadcast_to(jnp.exp(cum[count - 1 : count]), (8, 128))
    masked[...] = jnp.where(causal, dot(c_rows[...], b_t[...]), 0.0).astype(BF16)
    spread = (iota((heads, lanes_all), 1) // hd == iota((heads, lanes_all), 0)).astype(F32)
    skip_lanes[...] = jnp.dot(
        jnp.broadcast_to(skip_ref[...], (8, heads)), spread,
        preferred_element_type=F32, precision=lax.Precision.HIGHEST,
    )

    pl.semaphore_wait(barrier, PEERS - 1)

    def end_copy(d):
        peer = lax.rem(me + d, PEERS)
        return pltpu.make_async_remote_copy(
            src_ref=end_out, dst_ref=end_in.at[me], send_sem=end_send.at[d - 1],
            recv_sem=end_recv.at[d - 1], device_id={"tm": peer}, device_id_type=MESH,
        )

    def slice_copy(src, dst, send, recv, g, d):
        peer = lax.rem(me + d, PEERS)
        return pltpu.make_async_remote_copy(
            src_ref=src.at[g, peer], dst_ref=dst.at[g, me], send_sem=send.at[g, d - 1],
            recv_sem=recv.at[g, d - 1], device_id={"tm": peer}, device_id_type=MESH,
        )

    def each(do):
        def turn(d, carry):
            do(d)
            return carry

        lax.fori_loop(1, PEERS, turn, 0)

    each(lambda d: end_copy(d).start())
    end_in[pl.ds(me, 1)] = end_out[...][None]

    wide_rows = s_out.shape[3]
    many = wide_rows // LANES

    def project(i, g):
        j = g * per + i
        col = pl.multiple_of(j * 2 * LANES, 2 * LANES)
        at = pl.ds(pl.multiple_of(j * LANES, LANES), LANES)
        both = dot(normed[...], w_pair[:, pl.ds(col, 2 * LANES)]).astype(BF16).astype(F32)
        left = iota((count, 128), 1) < hd
        xs, zs = [], []
        for k in range(0, 2 * LANES, 256):
            v0, v1 = both[:, k : k + 128], both[:, k + 128 : k + 256]
            xs.append(jnp.where(left, v0, pltpu.roll(v1, hd, 1)))
            zs.append(jnp.where(left, pltpu.roll(v0, hd, 1), v1))
        x = jnp.concatenate(xs, axis=1)
        z = jnp.concatenate(zs, axis=1)
        row, lane = iota((128, 2 * LANES), 0), iota((128, 2 * LANES), 1)
        first = j * (LANES // hd)
        pick = (row % heads == first + (lane % LANES) // hd) & (row // (2 * heads) == lane // LANES)
        wide = dot(dec[...], pick.astype(F32).astype(BF16))
        grow = wide[:, :LANES]
        x_v[:, at] = x.astype(BF16)
        scaled = (x * wide[:, LANES:]).astype(BF16)
        xs_v[:, at] = scaled
        grow_v[:, at] = grow
        sz_v[:, at] = z * jax.nn.sigmoid(z)
        state = (dot(b_t[...], scaled) * grow[count - 1 : count]).astype(BF16)
        side = i // many
        inside = pl.ds(pl.multiple_of((i % many) * LANES, LANES), LANES)
        parts = PEERS * many // per
        s_out[g, pl.ds(side * parts, parts), :, inside] = state.reshape(
            parts, width // parts, LANES
        )

    def inner(i, g):
        at = pl.ds(pl.multiple_of((g * per + i) * LANES, LANES), LANES)
        cut = count // 2
        base = skip_lanes[0:1, at]
        top = dot(masked[:cut, :cut], xs_v[:cut, at])
        y_v[:cut, at] = top * grow_v[:cut, at] + base * x_v[:cut, at].astype(F32)
        low = dot(masked[cut:, :], xs_v[:, at])
        y_v[cut:, at] = low * grow_v[cut:, at] + base * x_v[cut:, at].astype(F32)

    def scan(g):
        each(lambda d: slice_copy(s_out, s_in, send1, recv1, g, d).wait_recv())
        s_in[g, pl.ds(me, 1)] = s_out[g, pl.ds(me, 1)]
        parts = PEERS * many // per
        side = me // parts
        first = (g * per + side * many) * (LANES // hd)
        pick = (
            iota((128, wide_rows), 0) == first + iota((128, wide_rows), 1) // hd
        ).astype(F32)
        ends = end_in[:, 0, :]
        decay = jnp.dot(ends, pick, preferred_element_type=F32, precision=lax.Precision.HIGHEST)
        running = jnp.zeros(s_in.shape[2:], F32)
        for k in range(PEERS):
            e_out[g, k] = running.astype(BF16)
            if k < PEERS - 1:
                running = decay[k : k + 1] * running + s_in[g, k].astype(F32)
        each(lambda d: slice_copy(e_out, e_in, send2, recv2, g, d).start())
        e_in[g, pl.ds(me, 1)] = e_out[g, pl.ds(me, 1)]

    def finish(i, g):
        at = pl.ds(pl.multiple_of((g * per + i) * LANES, LANES), LANES)
        parts = PEERS * many // per
        inside = pl.ds(pl.multiple_of((i % many) * LANES, LANES), LANES)
        state = e_in[g, pl.ds((i // many) * parts, parts), :, inside].reshape(width, LANES)
        y = y_v[:, at] + grow_v[:, at] * dot(c_rows[...], state)
        gated = y * sz_v[:, at]
        mean_of = jnp.where(
            iota((LANES, LANES), 0) // hd == iota((LANES, LANES), 1) // hd, 1.0 / hd, 0.0
        ).astype(BF16)
        mean = dot((gated * gated).astype(BF16), mean_of)
        mixed[:, at] = (gated * lax.rsqrt(mean + 1e-05) * out_gain_ref[:, at]).astype(BF16)

    def loop(do, n, g):
        def turn(i, carry):
            do(i, g)
            return carry

        lax.fori_loop(0, n, turn, 0)

    for g in range(GROUPS):
        loads[5 + g].wait()
        loop(project, per, g)
        each(lambda d: slice_copy(s_out, s_in, send1, recv1, g, d).start())
        if g == 0:
            each(lambda d: end_copy(d).wait_recv())
        else:
            scan(g - 1)
            loop(inner, per, g - 1)
    loop(inner, per, GROUPS - 1)
    scan(GROUPS - 1)
    loads[5 + GROUPS].wait()

    columns = 256
    deep = lanes_all // GROUPS
    for g in range(GROUPS):
        each(lambda d: slice_copy(e_out, e_in, send2, recv2, g, d).wait_recv())
        loop(finish, per, g)

        def merge(i, g):
            at = pl.ds(pl.multiple_of(i * columns, columns), columns)
            part = dot(mixed[:, pl.ds(g * deep, deep)], w_out[pl.ds(g * deep, deep), at])
            total = part + (encoded[:, at].astype(F32) if g == 0 else acc[:, at])
            if g < GROUPS - 1:
                acc[:, at] = total
            else:
                out_v[:, at] = total.astype(BF16)
                pltpu.make_async_copy(out_v.at[:, at], out_hbm.at[:, at], store_sem.at[i]).start()

        loop(merge, depth // columns, g)

    each(lambda d: end_copy(d).wait_send())
    for g in range(GROUPS):
        each(lambda d: slice_copy(s_out, s_in, send1, recv1, g, d).wait_send())
        each(lambda d: slice_copy(e_out, e_in, send2, recv2, g, d).wait_send())

    def stored(i, carry):
        at = pl.ds(pl.multiple_of(i * columns, columns), columns)
        pltpu.make_async_copy(out_v.at[:, at], out_hbm.at[:, at], store_sem.at[i]).wait()
        return carry

    lax.fori_loop(0, depth // columns, stored, 0)


def body(frames, patch_cell, enc_in, enc_bias, enc_out, pos_table, norm_gain, w_pair, w_keys,
         w_step, step_bias, decay_code, skip_gain, out_gain, w_out):
    count, pixels = frames.shape[0], frames.shape[2]
    depth = enc_out.shape[1]
    heads = w_step.shape[1]
    lanes = w_out.shape[0]
    width = w_keys.shape[1] // 2
    chunks = lanes // LANES
    per = chunks // GROUPS
    pos_row = lax.dynamic_slice_in_dim(pos_table, patch_cell[0], 1, 0)
    slice_rows = 16
    slice_lanes = width * per * LANES // (PEERS * slice_rows)
    comm = pltpu.VMEM((GROUPS, PEERS, slice_rows, slice_lanes), BF16)
    sems = pltpu.SemaphoreType.DMA((GROUPS, PEERS - 1))
    vm = pltpu.VMEM
    out = pl.pallas_call(
        kernel,
        out_shape=jax.ShapeDtypeStruct((count, depth), BF16),
        in_specs=[pl.BlockSpec(memory_space=pl.ANY)] * 7
        + [pl.BlockSpec(memory_space=pltpu.VMEM)] * 7,
        out_specs=pl.BlockSpec(memory_space=pl.ANY),
        scratch_shapes=[
            vm((count, pixels), BF16), vm((pixels, depth), BF16), vm((depth, depth), BF16),
            vm((depth, 2 * width), BF16), vm((depth, heads), BF16), vm((depth, 2 * lanes), BF16),
            vm((lanes, depth), BF16),
            vm((count, depth), BF16), vm((count, depth), BF16), vm((width, count), BF16),
            vm((count, width), BF16), vm((count, 128), BF16), vm((count, count), BF16),
            vm((count, lanes), BF16), vm((count, lanes), BF16), vm((count, lanes), F32),
            vm((count, lanes), F32), vm((count, lanes), F32), vm((count, depth), F32),
            vm((count, lanes), BF16), vm((count, depth), BF16), vm((8, lanes), F32),
            vm((8, 128), F32), vm((PEERS, 8, 128), F32), comm, comm, comm, comm,
            pltpu.SemaphoreType.DMA((6 + GROUPS,)), pltpu.SemaphoreType.DMA((depth // 256,)),
            pltpu.SemaphoreType.DMA((PEERS - 1,)), pltpu.SemaphoreType.DMA((PEERS - 1,)),
            sems, sems, sems, sems,
        ],
        compiler_params=pltpu.CompilerParams(
            collective_id=0, has_side_effects=True, vmem_limit_bytes=62 * 1024 * 1024
        ),
        name="layer",
    )(
        frames.reshape(count, pixels), enc_in, enc_out, w_keys, w_step, w_pair, w_out,
        pos_row, enc_bias[None], norm_gain[None], step_bias[None], decay_code[None],
        skip_gain[None], out_gain[None],
    )
    return out[:, None]


def solution(mesh):
    placed = (P("tm", "space", None), P("space")) + (P(),) * 13
    return jax.shard_map(
        body, mesh=mesh, in_specs=placed, out_specs=P("tm", "space", None), check_vma=False
    )
```

```python
import functools

import jax
import jax.numpy as jnp
from jax import lax
from jax.experimental import pallas as pl
from jax.experimental.pallas import tpu as pltpu
from jax.sharding import PartitionSpec as P

F32 = jnp.float32
BF16 = jnp.bfloat16
MESH = pl.DeviceIdType.MESH
GROUPS = 4
LANES = 256
PEERS = 16
ROWS = 128
VMEM_LIMIT = 60 * 1024 * 1024


def dot(a, b):
    return jnp.dot(a, b, preferred_element_type=F32)


def exact(a, b):
    return jnp.dot(a, b, preferred_element_type=F32, precision=lax.Precision.HIGHEST)


def iota(shape, axis):
    return lax.broadcasted_iota(jnp.int32, shape, axis)


def pipelined(first, second, blocks, third=None):
    first(0)
    for n in range(blocks):
        if n + 1 < blocks:
            first(n + 1)
        second(n)
        if third is not None and n > 0:
            third(n - 1)
    if third is not None:
        third(blocks - 1)


def kernel(
    frames_hbm, enc_in_hbm, enc_out_hbm, pos_hbm, w_keys_hbm, w_step_hbm, w_pair_hbm, w_out_hbm,
    cell_ref, enc_bias_ref, norm_gain_ref, step_bias_ref, code_ref, skip_ref, out_gain_ref,
    out_ref,
    frames, enc_in, enc_out, pos_table, w_keys, w_step, w_pair, w_out,
    hidden, raw, encoded, normed, step_w, step_v, b_t, c_rows, dec, masked,
    w_val, w_gate, x_v, xs_v, sz_v, grow_v, y_v, acc, mixed, skip_lanes,
    end_out, end_in, s_out, s_in, e_out, e_in,
    load_sem, end_send, end_recv, send1, recv1, send2, recv2,
):
    count, depth = encoded.shape
    heads = step_bias_ref.shape[1]
    width = c_rows.shape[1]
    lanes_all = x_v.shape[1]
    wide = lanes_all // GROUPS
    hd = lanes_all // heads
    me = lax.axis_index("tm")

    def pair_part(g):
        part = pl.ds(g * 2 * wide, 2 * wide)
        return (w_pair_hbm.at[:, part], w_pair.at[:, part])

    plan = [
        (frames_hbm, frames), (enc_in_hbm, enc_in), (enc_out_hbm, enc_out), (pos_hbm, pos_table),
        (w_keys_hbm, w_keys), (w_step_hbm, w_step),
    ]
    plan += [pair_part(g) for g in range(GROUPS)]
    plan.append((w_out_hbm, w_out))
    loads = [
        pltpu.make_async_copy(src, dst, load_sem.at[n]) for n, (src, dst) in enumerate(plan)
    ]
    for load in loads:
        load.start()

    barrier = pltpu.get_barrier_semaphore()

    def peer_at(d):
        return lax.rem(me + d, PEERS)

    for d in range(1, PEERS):
        pl.semaphore_signal(barrier, inc=1, device_id={"tm": peer_at(d)}, device_id_type=MESH)

    four = (iota((heads, 128), 1) % heads == iota((heads, 128), 0)).astype(F32)
    bias4 = exact(jnp.broadcast_to(step_bias_ref[...], (8, heads)), four)[:1]
    code4 = dot(jnp.broadcast_to(code_ref[...], (8, heads)).astype(BF16), four.astype(BF16))[:1]
    rate4 = -0.0005 - 0.003 * code4
    loads[0].wait()
    loads[1].wait()

    def hide(n):
        at = pl.ds(n * ROWS, ROWS)
        raw = dot(frames[at, :], enc_in[...]) + enc_bias_ref[...]
        hidden[at, :] = jax.nn.gelu(raw, approximate=True).astype(BF16)

    def draw(n):
        at = pl.ds(n * ROWS, ROWS)
        raw[at, :] = dot(hidden[at, :], enc_out[...])

    blocks = count // ROWS
    hide(0)
    hide(1)
    loads[2].wait()
    for n in range(blocks):
        draw(n)
        if n + 2 < blocks:
            hide(n + 2)

    for n in (3, 4, 5, 6):
        loads[n].wait()
    cell = cell_ref[0]
    near = pos_table[lax.div(cell, 16)].astype(F32)
    pos_row = jnp.sum(
        jnp.where(iota((16, depth), 0) == lax.rem(cell, 16), near, 0.0), axis=0, keepdims=True
    )
    step_w[...] = jnp.concatenate([w_step[...]] * (128 // heads), axis=0).T

    def pack(g):
        for k in range(g * (wide // 128), (g + 1) * (wide // 128)):
            v0 = w_pair[:, 256 * k : 256 * k + 128]
            v1 = pltpu.roll(w_pair[:, 256 * k + 128 : 256 * k + 256], hd, 1)
            left = iota((depth, 128), 1) < hd
            w_val[:, 128 * k : 128 * k + 128] = jnp.where(left, v0, v1)
            w_gate[:, 128 * k : 128 * k + 128] = jnp.where(left, v1, v0)

    def code(n):
        at = pl.ds(n * ROWS, ROWS)
        coded = (raw[at, :] + pos_row).astype(BF16)
        encoded[at, :] = coded
        plain = coded.astype(F32)
        mean = jnp.mean(plain * plain, axis=-1, keepdims=True)
        normed[at, :] = (plain * lax.rsqrt(mean + 1e-05) * norm_gain_ref[...]).astype(BF16)

    def key(n):
        at = pl.ds(n * ROWS, ROWS)
        keys = dot(normed[at, :], w_keys[...]).astype(BF16)
        b_t[:, at] = keys[:, :width].T
        c_rows[at, :] = keys[:, width:]
        step_v[at, :] = jax.nn.sigmoid(dot(normed[at, :], step_w[...]) + bias4).astype(BF16)

    pipelined(code, key, blocks)
    pack(0)

    half = count // 2
    lane = iota((half, 128), 1)
    for top, deep in ((0, half), (half, count)):
        causal = iota((half, deep), 0) + top >= iota((half, deep), 1)
        cum = dot(causal.astype(F32).astype(BF16), step_v[:deep, :]) * rate4
        high = cum.astype(BF16).astype(F32)
        mid = (cum - high).astype(BF16).astype(F32)
        low = cum - high - mid
        part = lane // heads
        dec[top : top + half, :] = jnp.where(
            part == 0, high, jnp.where(part == 1, mid, jnp.where(part == 2, low, 0.0))
        ).astype(BF16)
    end_out[...] = jnp.broadcast_to(jnp.exp(cum[half - 1 : half]), (8, 128))

    pl.semaphore_wait(barrier, PEERS - 1)

    def end_copy(d, n=None):
        return pltpu.make_async_remote_copy(
            src_ref=end_out if n is None else end_in.at[pl.ds(0, n)],
            dst_ref=end_in.at[me] if n is None else end_in.at[pl.ds(0, n)],
            send_sem=end_send, recv_sem=end_recv, device_id={"tm": peer_at(d)}, device_id_type=MESH,
        )

    def slice_copy(src, dst, send, recv, g, d):
        return pltpu.make_async_remote_copy(
            src_ref=src.at[g, peer_at(d)], dst_ref=dst.at[g, me], send_sem=send.at[g],
            recv_sem=recv.at[g], device_id={"tm": peer_at(d)}, device_id_type=MESH,
        )

    def all_copies(src, dst, send, recv, g):
        every = pl.ds(0, PEERS - 1)
        return pltpu.make_async_remote_copy(
            src_ref=src.at[g, every], dst_ref=dst.at[g, every], send_sem=send.at[g],
            recv_sem=recv.at[g], device_id={"tm": peer_at(1)}, device_id_type=MESH,
        )

    for d in range(1, PEERS):
        end_copy(d).start()
    end_in[pl.ds(me, 1)] = end_out[...][None]

    sides = wide // LANES
    parts = PEERS // sides
    rows = width // parts

    def values(g):
        if g + 1 < GROUPS:
            loads[7 + g].wait()
        at = pl.ds(g * wide, wide)
        x = dot(normed[...], w_val[:, at]).astype(BF16)
        x_v[:, at] = x
        row, lane = iota((128, wide), 0), iota((128, wide), 1)
        pick = (row % heads == g * (wide // hd) + lane // hd) & (row < 3 * heads)
        cum = dot(dec[...], pick.astype(F32).astype(BF16))
        grow = jnp.exp(cum)
        grow_v[:, at] = grow
        scaled = (x.astype(F32) * jnp.exp(-cum)).astype(BF16)
        xs_v[:, at] = scaled
        state = (dot(b_t[...], scaled) * grow[count - 1 : count]).astype(BF16)
        for side in range(sides):
            s_out[g, pl.ds(side * parts, parts)] = state[
                :, side * LANES : (side + 1) * LANES
            ].reshape(parts, rows, LANES)
        if g + 1 < GROUPS:
            pack(g + 1)
        for d in range(1, PEERS):
            slice_copy(s_out, s_in, send1, recv1, g, d).start()

    def gates(g):
        at = pl.ds(g * wide, wide)
        z = dot(normed[...], w_gate[:, at]).astype(BF16).astype(F32)
        z = z * jax.nn.sigmoid(z)
        for k in range(wide // 128):
            sz_v[:, pl.ds(g * wide + 128 * k, 128)] = pltpu.roll(z[:, 128 * k : 128 * k + 128], hd, 1)

    def inner(g):
        at = pl.ds(g * wide, wide)
        base = skip_lanes[0:1, at]
        for top, deep in ((0, half), (half, count)):
            here = pl.ds(top, half)
            sums = dot(masked[here, :deep], xs_v[:deep, at])
            y_v[here, at] = sums * grow_v[here, at] + base * x_v[here, at].astype(F32)

    def scan(g):
        first = (g * sides + me // parts) * (LANES // hd)
        pick = (iota((128, LANES), 0) == first + iota((128, LANES), 1) // hd).astype(F32)
        decay = exact(end_in[:, 0, :], pick)
        all_copies(s_out, s_in, send1, recv1, g).wait_recv()
        s_in[g, pl.ds(me, 1)] = s_out[g, pl.ds(me, 1)]
        running = jnp.zeros(s_in.shape[2:], F32)
        for k in range(PEERS):
            e_out[g, k] = running.astype(BF16)
            if k < PEERS - 1:
                running = decay[k : k + 1] * running + s_in[g, k].astype(F32)
        for d in range(1, PEERS):
            slice_copy(e_out, e_in, send2, recv2, g, d).start()
        e_in[g, pl.ds(me, 1)] = e_out[g, pl.ds(me, 1)]

    mean_of = jnp.where(
        iota((LANES, LANES), 0) // hd == iota((LANES, LANES), 1) // hd, 1.0 / hd, 0.0
    ).astype(BF16)

    def finish(g, n):
        here = pl.ds(n * ROWS, ROWS)
        for side in range(sides):
            at = pl.ds(g * wide + side * LANES, LANES)
            state = e_in[g, pl.ds(side * parts, parts)].reshape(width, LANES)
            y = y_v[here, at] + grow_v[here, at] * dot(c_rows[here, :], state)
            gated = y * sz_v[here, at]
            mean = dot((gated * gated).astype(BF16), mean_of)
            mixed[here, at] = (gated * lax.rsqrt(mean + 1e-05) * out_gain_ref[:, at]).astype(BF16)

    def merge(g, n):
        here = pl.ds(n * ROWS, ROWS)
        at = pl.ds(g * wide, wide)
        part = dot(mixed[here, at], w_out[at, :])
        total = part + (encoded[here, :].astype(F32) if g == 0 else acc[here, :])
        if g < GROUPS - 1:
            acc[here, :] = total
        else:
            out_ref[here, :] = total.astype(BF16)

    for g in range(GROUPS):
        values(g)
    end_copy(1, PEERS - 1).wait_recv()
    spread = (iota((heads, lanes_all), 1) // hd == iota((heads, lanes_all), 0)).astype(F32)
    skip_lanes[...] = exact(jnp.broadcast_to(skip_ref[...], (8, heads)), spread)
    gates(0)
    gates(1)
    for top, deep in ((0, half), (half, count)):
        causal = iota((half, deep), 0) + top >= iota((half, deep), 1)
        masked[top : top + half, :deep] = jnp.where(
            causal, dot(c_rows[top : top + half, :], b_t[:, :deep]), 0.0
        ).astype(BF16)
    scan(0)
    gates(2)
    inner(0)
    scan(1)
    gates(3)
    inner(1)
    scan(2)
    inner(2)
    inner(3)
    scan(3)
    loads[6 + GROUPS].wait()
    for g in range(GROUPS):
        all_copies(e_out, e_in, send2, recv2, g).wait_recv()
        pipelined(functools.partial(finish, g), functools.partial(merge, g), blocks)

    end_copy(1, PEERS - 1).wait_send()
    for g in range(GROUPS):
        all_copies(s_out, s_in, send1, recv1, g).wait_send()
        all_copies(e_out, e_in, send2, recv2, g).wait_send()


def body(frames, patch_cell, enc_in, enc_bias, enc_out, pos_table, norm_gain, w_pair, w_keys,
         w_step, step_bias, decay_code, skip_gain, out_gain, w_out):
    count, pixels = frames.shape[0], frames.shape[2]
    depth = enc_out.shape[1]
    heads = w_step.shape[1]
    lanes = w_out.shape[0]
    width = w_keys.shape[1] // 2
    slice_rows = width * lanes // (GROUPS * PEERS * LANES)
    vm = pltpu.VMEM
    comm = vm((GROUPS, PEERS, slice_rows, LANES), BF16)
    dma = pltpu.SemaphoreType.DMA
    out = pl.pallas_call(
        kernel,
        out_shape=jax.ShapeDtypeStruct((count, depth), BF16),
        in_specs=[pl.BlockSpec(memory_space=pl.ANY)] * 8
        + [pl.BlockSpec(memory_space=pltpu.SMEM)]
        + [pl.BlockSpec(memory_space=pltpu.VMEM)] * 6,
        out_specs=pl.BlockSpec(memory_space=pltpu.VMEM),
        scratch_shapes=[
            vm((count, pixels), BF16), vm((pixels, depth), BF16), vm((depth, depth), BF16),
            vm((pos_table.shape[0] // 16, 16, depth), BF16), vm((depth, 2 * width), BF16), vm((heads, depth), BF16),
            vm((depth, 2 * lanes), BF16), vm((lanes, depth), BF16),
            vm((count, depth), BF16), vm((count, depth), F32), vm((count, depth), BF16),
            vm((count, depth), BF16), vm((depth, 128), BF16), vm((count, 128), BF16), vm((width, count), BF16),
            vm((count, width), BF16), vm((count, 128), BF16), vm((count, count), BF16),
            vm((depth, lanes), BF16), vm((depth, lanes), BF16), vm((count, lanes), BF16),
            vm((count, lanes), BF16),
            vm((count, lanes), F32), vm((count, lanes), F32), vm((count, lanes), F32),
            vm((count, depth), F32), vm((count, lanes), BF16), vm((8, lanes), F32),
            vm((8, 128), F32), vm((PEERS, 8, 128), F32), comm, comm, comm, comm,
            dma((7 + GROUPS,)), dma, dma,
            dma((GROUPS,)), dma((GROUPS,)), dma((GROUPS,)), dma((GROUPS,)),
        ],
        compiler_params=pltpu.CompilerParams(
            collective_id=0, has_side_effects=True, vmem_limit_bytes=VMEM_LIMIT
        ),
        name="layer",
    )(
        frames.reshape(count, pixels), enc_in, enc_out,
        pos_table.reshape(pos_table.shape[0] // 16, 16, depth), w_keys, w_step.T, w_pair, w_out,
        patch_cell, enc_bias[None], norm_gain[None], step_bias[None], decay_code[None],
        skip_gain[None], out_gain[None],
    )
    return out[:, None]


def solution(mesh):
    placed = (P("tm", "space", None), P("space")) + (P(),) * 13
    return jax.shard_map(
        body, mesh=mesh, in_specs=placed, out_specs=P("tm", "space", None), check_vma=False
    )
```

```python
import functools

import jax
import jax.numpy as jnp
from jax import lax
from jax.experimental import pallas as pl
from jax.experimental.pallas import tpu as pltpu
from jax.sharding import PartitionSpec as P

F32 = jnp.float32
BF16 = jnp.bfloat16
MESH = pl.DeviceIdType.MESH
SIZES = (512, 768, 512, 256)
GROUPS = len(SIZES)
STARTS = tuple(sum(SIZES[:g]) for g in range(GROUPS))
PARTS = 8
PEERS = 16
ROWS = 128
BIG = 256
VMEM_LIMIT = 54 * 1024 * 1024


def dot(a, b):
    return jnp.dot(a, b, preferred_element_type=F32)


def exact(a, b):
    return jnp.dot(a, b, preferred_element_type=F32, precision=lax.Precision.HIGHEST)


def iota(shape, axis):
    return lax.broadcasted_iota(jnp.int32, shape, axis)


def pipelined(first, second, blocks, third=None):
    first(0)
    for n in range(blocks):
        if n + 1 < blocks:
            first(n + 1)
        second(n)
        if third is not None and n > 0:
            third(n - 1)
    if third is not None:
        third(blocks - 1)


def kernel(
    frames_hbm, enc_in_hbm, enc_out_hbm, pos_hbm, w_keys_hbm, w_step_hbm, w_pair_hbm, w_out_hbm,
    cell_ref, enc_bias_ref, norm_gain_ref, step_bias_ref, code_ref, skip_ref, out_gain_ref,
    out_hbm,
    frames, enc_in, enc_out, pos_table, w_keys, w_step, w_pair, w_out,
    hidden, encoded, normed, step_w, step_v, b_t, c_rows, dec, masked,
    w_val, w_gate, x_v, xs_v, sz_v, grow_v, y_v, acc, mixed, skip_lanes,
    out_v, end_out, end_in, *rest,
):
    count, depth = encoded.shape
    heads = step_bias_ref.shape[1]
    width = c_rows.shape[1]
    lanes_all = x_v.shape[1]
    s_out, s_in, e_out, e_in = (rest[k * GROUPS : (k + 1) * GROUPS] for k in range(4))
    load_sem, store_sem, end_send, end_recv, send1, recv1, send2, recv2 = rest[4 * GROUPS :]
    hd = lanes_all // heads
    me = lax.axis_index("tm")

    def pair_part(g):
        part = pl.ds(2 * STARTS[g], 2 * SIZES[g])
        return (w_pair_hbm.at[:, part], w_pair.at[:, part])

    plan = [
        (frames_hbm, frames), (enc_in_hbm, enc_in), (enc_out_hbm, enc_out), (pos_hbm, pos_table),
        (w_keys_hbm, w_keys), (w_step_hbm, w_step),
    ]
    plan += [pair_part(g) for g in range(GROUPS)]
    plan.append((w_out_hbm, w_out))
    loads = [
        pltpu.make_async_copy(src, dst, load_sem.at[n]) for n, (src, dst) in enumerate(plan)
    ]
    for load in loads:
        load.start()

    barrier = pltpu.get_barrier_semaphore()

    def peer_at(d):
        return lax.rem(me + d, PEERS)

    for d in range(1, PEERS):
        pl.semaphore_signal(barrier, inc=1, device_id={"tm": peer_at(d)}, device_id_type=MESH)

    four = (iota((heads, 128), 1) % heads == iota((heads, 128), 0)).astype(F32)
    bias4 = exact(jnp.broadcast_to(step_bias_ref[...], (8, heads)), four)[:1]
    code4 = dot(jnp.broadcast_to(code_ref[...], (8, heads)).astype(BF16), four.astype(BF16))[:1]
    rate4 = (-0.0005 - 0.003 * code4) * 1.4426950408889634
    loads[0].wait()
    loads[1].wait()

    def hide(n):
        at = pl.ds(n * BIG, BIG)
        raw = dot(frames[at, :], enc_in[...]) + enc_bias_ref[...]
        near = 0.5 * raw
        bent = jnp.tanh(raw * (0.7978845608028654 + 0.035677408136300125 * (raw * raw)))
        hidden[at, :] = (near + near * bent).astype(BF16)

    def draw(n):
        at = pl.ds(n * BIG, BIG)
        acc[at, :] = dot(hidden[at, :], enc_out[...])

    hide(0)
    loads[2].wait()
    pipelined(lambda n: hide(n) if n else None, draw, count // BIG)

    for n in (3, 4, 5, 6):
        loads[n].wait()
    cell = cell_ref[0]
    near = pos_table[lax.div(cell, 16)].astype(F32)
    pos_row = jnp.sum(
        jnp.where(iota((16, depth), 0) == lax.rem(cell, 16), near, 0.0), axis=0, keepdims=True
    )
    step_w[...] = jnp.concatenate([w_step[...]] * (128 // heads), axis=0).T

    def pack(first, last):
        for k in range(first, last):
            v0 = w_pair[:, 256 * k : 256 * k + 128]
            v1 = pltpu.roll(w_pair[:, 256 * k + 128 : 256 * k + 256], hd, 1)
            left = iota((depth, 128), 1) < hd
            w_val[:, 128 * k : 128 * k + 128] = jnp.where(left, v0, v1)
            w_gate[:, 128 * k : 128 * k + 128] = jnp.where(left, v1, v0)

    def code(n):
        at = pl.ds(n * ROWS, ROWS)
        coded = (acc[at, :] + pos_row).astype(BF16)
        encoded[at, :] = coded
        plain = coded.astype(F32)
        mean = jnp.mean(plain * plain, axis=-1, keepdims=True)
        normed[at, :] = (plain * lax.rsqrt(mean + 1e-05) * norm_gain_ref[...]).astype(BF16)

    def key(n):
        at = pl.ds(n * BIG, BIG)
        keys = dot(normed[at, :], w_keys[...]).astype(BF16)
        b_t[:, at] = keys[:, :width].T
        c_rows[at, :] = keys[:, width:]
        step_v[at, :] = jax.nn.sigmoid(dot(normed[at, :], step_w[...]) + bias4).astype(BF16)

    blocks = count // ROWS
    each = BIG // ROWS
    pack(0, SIZES[0] // 128)
    pipelined(lambda n: [code(n * each + k) for k in range(each)], key, count // BIG)

    half = count // 2
    lane = iota((half, 128), 1)
    for top, deep in ((0, half), (half, count)):
        causal = iota((half, deep), 0) + top >= iota((half, deep), 1)
        cum = dot(causal.astype(F32).astype(BF16), step_v[:deep, :]) * rate4
        high = cum.astype(BF16).astype(F32)
        mid = (cum - high).astype(BF16).astype(F32)
        low = cum - high - mid
        part = lane // heads
        dec[top : top + half, :] = jnp.where(
            part == 0, high, jnp.where(part == 1, mid, jnp.where(part == 2, low, 0.0))
        ).astype(BF16)
    end_out[...] = jnp.broadcast_to(jnp.exp2(cum[half - 1 : half]), (8, 128))

    pl.semaphore_wait(barrier, PEERS - 1)

    def end_copy(d, n=None):
        return pltpu.make_async_remote_copy(
            src_ref=end_out if n is None else end_in.at[pl.ds(0, n)],
            dst_ref=end_in.at[me] if n is None else end_in.at[pl.ds(0, n)],
            send_sem=end_send, recv_sem=end_recv, device_id={"tm": peer_at(d)}, device_id_type=MESH,
        )

    def slice_copy(src, dst, send, recv, g, d):
        return pltpu.make_async_remote_copy(
            src_ref=src[g].at[peer_at(d)], dst_ref=dst[g].at[me], send_sem=send.at[g],
            recv_sem=recv.at[g], device_id={"tm": peer_at(d)}, device_id_type=MESH,
        )

    def all_copies(src, dst, send, recv, g):
        every = pl.ds(0, PEERS - 1)
        return pltpu.make_async_remote_copy(
            src_ref=src[g].at[every], dst_ref=dst[g].at[every], send_sem=send.at[g],
            recv_sem=recv.at[g], device_id={"tm": peer_at(1)}, device_id_type=MESH,
        )

    for d in range(1, PEERS):
        end_copy(d).start()
    end_in[pl.ds(me, 1)] = end_out[...][None]

    rows = width // PARTS
    sides = PEERS // PARTS

    def values(g):
        if g + 1 < GROUPS:
            loads[7 + g].wait()
            pack(STARTS[g + 1] // 128, (STARTS[g + 1] + SIZES[g + 1]) // 128)
        base, wide = STARTS[g], SIZES[g]
        at = pl.ds(base, wide)
        row, lane = iota((128, wide), 0), iota((128, wide), 1)
        pick = (row % heads == base // hd + lane // hd) & (row < 3 * heads)
        pick = pick.astype(F32).astype(BF16)
        held[g] = dot(dec[...], pick), dot(normed[...], w_val[:, at])

    def scale(g):
        wide = SIZES[g]
        at = pl.ds(STARTS[g], wide)
        cum, x = held.pop(g)
        grow_v[:, at] = jnp.exp2(cum)
        x_v[:, at] = x.astype(BF16)
        xs_v[:, at] = (x * jnp.exp2(-cum)).astype(BF16)
        state = (dot(b_t[...], xs_v[:, at]) * grow_v[count - 1 : count, at]).astype(BF16)
        for side in range(sides):
            lanes = wide // sides
            s_out[g][pl.ds(side * PARTS, PARTS)] = state[
                :, side * lanes : (side + 1) * lanes
            ].reshape(PARTS, rows, lanes)
        for d in range(1, PEERS):
            slice_copy(s_out, s_in, send1, recv1, g, d).start()

    def gates(g):
        held[g] = dot(normed[...], w_gate[:, pl.ds(STARTS[g], SIZES[g])]).astype(BF16).astype(F32)

    def swish(g):
        z = held.pop(g)
        z = z * jax.nn.sigmoid(z)
        for k in range(SIZES[g] // 128):
            sz_v[:, pl.ds(STARTS[g] + 128 * k, 128)] = pltpu.roll(z[:, 128 * k : 128 * k + 128], hd, 1)

    def inner(g):
        at = pl.ds(STARTS[g], SIZES[g])
        for n in range(count // BIG):
            here = pl.ds(n * BIG, BIG)
            deep = (n + 1) * BIG
            sums = dot(masked[here, :deep], xs_v[:deep, at])
            y_v[here, at] = sums * grow_v[here, at] + skip_lanes[0:1, at] * x_v[here, at].astype(F32)

    def scan(g):
        lanes = SIZES[g] // sides
        first = STARTS[g] // hd + (me // PARTS) * (lanes // hd)
        pick = (iota((128, lanes), 0) == first + iota((128, lanes), 1) // hd).astype(F32)
        decay = exact(end_in[:, 0, :], pick)
        all_copies(s_out, s_in, send1, recv1, g).wait_recv()
        s_in[g][pl.ds(me, 1)] = s_out[g][pl.ds(me, 1)]
        running = jnp.zeros((rows, lanes), F32)
        for k in range(PEERS):
            e_out[g][k] = running.astype(BF16)
            if k < PEERS - 1:
                running = decay[k : k + 1] * running + s_in[g][k].astype(F32)
        for d in range(1, PEERS):
            slice_copy(e_out, e_in, send2, recv2, g, d).start()
        e_in[g][pl.ds(me, 1)] = e_out[g][pl.ds(me, 1)]

    square = 256
    mean_of = jnp.where(
        iota((square, square), 0) // hd == iota((square, square), 1) // hd, 1.0 / hd, 0.0
    ).astype(BF16)

    def merge(g, here, cols):
        at = pl.ds(STARTS[g], SIZES[g])
        part = dot(mixed[here, at], w_out[at, cols])
        total = part + (encoded[here, cols].astype(F32) if g == 0 else acc[here, cols])
        if g < GROUPS - 1:
            acc[here, cols] = total
        else:
            out_v[here, cols] = total.astype(BF16)

    def finish(g):
        every, middle = pl.ds(0, count), depth // 2
        wide = SIZES[g]
        state = jnp.concatenate(
            [e_in[g][pl.ds(side * PARTS, PARTS)].reshape(width, wide // sides) for side in range(sides)],
            axis=1,
        )
        carried = dot(c_rows[...], state)
        if g:
            merge(g - 1, every, pl.ds(0, middle))
        means = []
        for k in range(0, wide, square):
            at = pl.ds(STARTS[g] + k, square)
            gated = (y_v[:, at] + grow_v[:, at] * carried[:, k : k + square]) * sz_v[:, at]
            y_v[:, at] = gated
            means.append(dot((gated * gated).astype(BF16), mean_of))
        if g:
            merge(g - 1, every, pl.ds(middle, middle))
        for k in range(0, wide, square):
            at = pl.ds(STARTS[g] + k, square)
            root = lax.rsqrt(means[k // square] + 1e-05)
            mixed[:, at] = (y_v[:, at] * root * out_gain_ref[:, at]).astype(BF16)

    held = {}
    for g in range(GROUPS):
        values(g)
        scale(g)
    end_copy(1, PEERS - 1).wait_recv()
    spread = (iota((heads, lanes_all), 1) // hd == iota((heads, lanes_all), 0)).astype(F32)
    skip_lanes[...] = exact(jnp.broadcast_to(skip_ref[...], (8, heads)), spread)
    def mask(n):
        here, deep = pl.ds(n * BIG, BIG), (n + 1) * BIG
        causal = iota((BIG, deep), 0) + n * BIG >= iota((BIG, deep), 1)
        masked[here, :deep] = jnp.where(causal, dot(c_rows[here, :], b_t[:, :deep]), 0.0).astype(BF16)

    gates(0)
    gates(1)
    swish(0)
    for n in range(count // BIG):
        mask(n)
    swish(1)
    scan(0)
    gates(2)
    inner(0)
    swish(2)
    scan(1)
    gates(3)
    inner(1)
    swish(3)
    scan(2)
    inner(2)
    inner(3)
    scan(3)
    loads[6 + GROUPS].wait()
    for g in range(GROUPS):
        all_copies(e_out, e_in, send2, recv2, g).wait_recv()
        finish(g)

    def store(n):
        here = pl.ds(n * ROWS, ROWS)
        return pltpu.make_async_copy(out_v.at[here], out_hbm.at[here], store_sem.at[n])

    for n in range(blocks):
        merge(GROUPS - 1, pl.ds(n * ROWS, ROWS), pl.ds(0, depth))
        store(n).start()

    end_copy(1, PEERS - 1).wait_send()
    for g in range(GROUPS):
        all_copies(s_out, s_in, send1, recv1, g).wait_send()
        all_copies(e_out, e_in, send2, recv2, g).wait_send()

    for n in range(blocks):
        store(n).wait()


def body(frames, patch_cell, enc_in, enc_bias, enc_out, pos_table, norm_gain, w_pair, w_keys,
         w_step, step_bias, decay_code, skip_gain, out_gain, w_out):
    count, pixels = frames.shape[0], frames.shape[2]
    depth = enc_out.shape[1]
    heads = w_step.shape[1]
    lanes = w_out.shape[0]
    width = w_keys.shape[1] // 2
    vm = pltpu.VMEM
    comm = [vm((PEERS, width // PARTS, wide * PARTS // PEERS), BF16) for wide in SIZES]
    dma = pltpu.SemaphoreType.DMA
    out = pl.pallas_call(
        kernel,
        out_shape=jax.ShapeDtypeStruct((count, depth), BF16),
        in_specs=[pl.BlockSpec(memory_space=pltpu.HBM)] * 8
        + [pl.BlockSpec(memory_space=pltpu.SMEM)]
        + [pl.BlockSpec(memory_space=pltpu.VMEM)] * 6,
        out_specs=pl.BlockSpec(memory_space=pl.ANY),
        scratch_shapes=[
            vm((count, pixels), BF16), vm((pixels, depth), BF16), vm((depth, depth), BF16),
            vm((pos_table.shape[0] // 16, 16, depth), BF16), vm((depth, 2 * width), BF16), vm((heads, depth), BF16),
            vm((depth, 2 * lanes), BF16), vm((lanes, depth), BF16),
            vm((count, depth), BF16), vm((count, depth), BF16),
            vm((count, depth), BF16), vm((depth, 128), BF16), vm((count, 128), BF16), vm((width, count), BF16),
            vm((count, width), BF16), vm((count, 128), BF16), vm((count, count), BF16),
            vm((depth, lanes), BF16), vm((depth, lanes), BF16), vm((count, lanes), BF16),
            vm((count, lanes), BF16),
            vm((count, lanes), F32), vm((count, lanes), F32), vm((count, lanes), F32),
            vm((count, depth), F32), vm((count, lanes), BF16), vm((8, lanes), F32),
            vm((count, depth), BF16), vm((8, 128), F32), vm((PEERS, 8, 128), F32), *comm * 4,
            dma((7 + GROUPS,)), dma((count // ROWS,)), dma, dma,
            dma((GROUPS,)), dma((GROUPS,)), dma((GROUPS,)), dma((GROUPS,)),
        ],
        compiler_params=pltpu.CompilerParams(
            collective_id=0, has_side_effects=True, vmem_limit_bytes=VMEM_LIMIT
        ),
        name="layer",
    )(
        frames.reshape(count, pixels), enc_in, enc_out,
        pos_table.reshape(pos_table.shape[0] // 16, 16, depth), w_keys, w_step.T, w_pair, w_out,
        patch_cell, enc_bias[None], norm_gain[None], step_bias[None], decay_code[None],
        skip_gain[None], out_gain[None],
    )
    return out[:, None]


def solution(mesh):
    placed = (P("tm", "space", None), P("space")) + (P(),) * 13
    return jax.shard_map(
        body, mesh=mesh, in_specs=placed, out_specs=P("tm", "space", None), check_vma=False
    )
```

```python
import functools

import jax
import jax.numpy as jnp
from jax import lax
from jax.experimental import pallas as pl
from jax.experimental.pallas import tpu as pltpu
from jax.sharding import PartitionSpec as P

F32 = jnp.float32
BF16 = jnp.bfloat16
MESH = pl.DeviceIdType.MESH
GROUPS = 4
LANES = 256
PEERS = 16
ROWS = 256
BIG = 256
VMEM_LIMIT = 54 * 1024 * 1024


def dot(a, b):
    return jnp.dot(a, b, preferred_element_type=F32)


def exact(a, b):
    return jnp.dot(a, b, preferred_element_type=F32, precision=lax.Precision.HIGHEST)


def iota(shape, axis):
    return lax.broadcasted_iota(jnp.int32, shape, axis)


def pipelined(first, second, blocks, third=None):
    first(0)
    for n in range(blocks):
        if n + 1 < blocks:
            first(n + 1)
        second(n)
        if third is not None and n > 0:
            third(n - 1)
    if third is not None:
        third(blocks - 1)


def kernel(
    frames_hbm, enc_in_hbm, enc_out_hbm, pos_hbm, w_keys_hbm, w_step_hbm, w_pair_hbm, w_out_hbm,
    cell_ref, enc_bias_ref, norm_gain_ref, step_bias_ref, code_ref, skip_ref, out_gain_ref,
    out_hbm,
    frames, enc_in, enc_out, pos_table, w_keys, w_step, w_pair, w_out,
    hidden, encoded, normed, step_w, step_v, b_t, c_rows, dec, masked,
    w_val, w_gate, x_v, xs_v, sz_v, grow_v, y_v, acc, mixed, skip_lanes,
    out_v, end_out, end_in, s_out, s_in, e_out, e_in,
    load_sem, store_sem, end_send, end_recv, send1, recv1, send2, recv2,
):
    count, depth = encoded.shape
    heads = step_bias_ref.shape[1]
    width = c_rows.shape[1]
    lanes_all = x_v.shape[1]
    wide = lanes_all // GROUPS
    hd = lanes_all // heads
    me = lax.axis_index("tm")

    def pair_part(g):
        part = pl.ds(g * 2 * wide, 2 * wide)
        return (w_pair_hbm.at[:, part], w_pair.at[:, part])

    plan = [
        (frames_hbm, frames), (enc_in_hbm, enc_in), (enc_out_hbm, enc_out), (pos_hbm, pos_table),
        (w_keys_hbm, w_keys), (w_step_hbm, w_step),
    ]
    plan += [pair_part(g) for g in range(GROUPS)]
    plan.append((w_out_hbm, w_out))
    loads = [
        pltpu.make_async_copy(src, dst, load_sem.at[n]) for n, (src, dst) in enumerate(plan)
    ]
    for load in loads:
        load.start()

    barrier = pltpu.get_barrier_semaphore()

    def peer_at(d):
        return lax.rem(me + d, PEERS)

    for d in range(1, PEERS):
        pl.semaphore_signal(barrier, inc=1, device_id={"tm": peer_at(d)}, device_id_type=MESH)

    four = (iota((heads, 128), 1) % heads == iota((heads, 128), 0)).astype(F32)
    bias4 = exact(jnp.broadcast_to(step_bias_ref[...], (8, heads)), four)[:1]
    code4 = dot(jnp.broadcast_to(code_ref[...], (8, heads)).astype(BF16), four.astype(BF16))[:1]
    rate4 = (-0.0005 - 0.003 * code4) * 1.4426950408889634
    loads[0].wait()
    loads[1].wait()

    def hide(n):
        at = pl.ds(n * BIG, BIG)
        raw = dot(frames[at, :], enc_in[...]) + enc_bias_ref[...]
        near = 0.5 * raw
        bent = jnp.tanh(raw * (0.7978845608028654 + 0.035677408136300125 * (raw * raw)))
        hidden[at, :] = (near + near * bent).astype(BF16)

    def draw(n):
        at = pl.ds(n * BIG, BIG)
        acc[at, :] = dot(hidden[at, :], enc_out[...])

    hide(0)
    loads[2].wait()
    pipelined(lambda n: hide(n) if n else None, draw, count // BIG)

    for n in (3, 4, 5, 6):
        loads[n].wait()
    cell = cell_ref[0]
    near = pos_table[lax.div(cell, 16)].astype(F32)
    pos_row = jnp.sum(
        jnp.where(iota((16, depth), 0) == lax.rem(cell, 16), near, 0.0), axis=0, keepdims=True
    )
    step_w[...] = jnp.concatenate([w_step[...]] * (128 // heads), axis=0).T

    def pack(first, last):
        for k in range(first, last):
            v0 = w_pair[:, 256 * k : 256 * k + 128]
            v1 = pltpu.roll(w_pair[:, 256 * k + 128 : 256 * k + 256], hd, 1)
            left = iota((depth, 128), 1) < hd
            w_val[:, 128 * k : 128 * k + 128] = jnp.where(left, v0, v1)
            w_gate[:, 128 * k : 128 * k + 128] = jnp.where(left, v1, v0)

    def code(n):
        at = pl.ds(n * ROWS, ROWS)
        coded = (acc[at, :] + pos_row).astype(BF16)
        encoded[at, :] = coded
        plain = coded.astype(F32)
        mean = jnp.mean(plain * plain, axis=-1, keepdims=True)
        normed[at, :] = (plain * lax.rsqrt(mean + 1e-05) * norm_gain_ref[...]).astype(BF16)

    def key(n):
        at = pl.ds(n * BIG, BIG)
        keys = dot(normed[at, :], w_keys[...]).astype(BF16)
        b_t[:, at] = keys[:, :width].T
        c_rows[at, :] = keys[:, width:]
        step_v[at, :] = jax.nn.sigmoid(dot(normed[at, :], step_w[...]) + bias4).astype(BF16)

    blocks = count // ROWS
    each = BIG // ROWS
    pack(0, wide // 128)
    pipelined(lambda n: [code(n * each + k) for k in range(each)], key, count // BIG)

    half = count // 2
    lane = iota((half, 128), 1)
    for top, deep in ((0, half), (half, count)):
        causal = iota((half, deep), 0) + top >= iota((half, deep), 1)
        cum = dot(causal.astype(F32).astype(BF16), step_v[:deep, :]) * rate4
        high = cum.astype(BF16).astype(F32)
        mid = (cum - high).astype(BF16).astype(F32)
        low = cum - high - mid
        part = lane // heads
        dec[top : top + half, :] = jnp.where(
            part == 0, high, jnp.where(part == 1, mid, jnp.where(part == 2, low, 0.0))
        ).astype(BF16)
    end_out[...] = jnp.broadcast_to(jnp.exp2(cum[half - 1 : half]), (8, 128))

    pl.semaphore_wait(barrier, PEERS - 1)

    def end_copy(d, n=None):
        return pltpu.make_async_remote_copy(
            src_ref=end_out if n is None else end_in.at[pl.ds(0, n)],
            dst_ref=end_in.at[me] if n is None else end_in.at[pl.ds(0, n)],
            send_sem=end_send, recv_sem=end_recv, device_id={"tm": peer_at(d)}, device_id_type=MESH,
        )

    def slice_copy(src, dst, send, recv, g, d):
        return pltpu.make_async_remote_copy(
            src_ref=src.at[g, peer_at(d)], dst_ref=dst.at[g, me], send_sem=send.at[g],
            recv_sem=recv.at[g], device_id={"tm": peer_at(d)}, device_id_type=MESH,
        )

    def all_copies(src, dst, send, recv, g):
        every = pl.ds(0, PEERS - 1)
        return pltpu.make_async_remote_copy(
            src_ref=src.at[g, every], dst_ref=dst.at[g, every], send_sem=send.at[g],
            recv_sem=recv.at[g], device_id={"tm": peer_at(1)}, device_id_type=MESH,
        )

    for d in range(1, PEERS):
        end_copy(d).start()
    end_in[pl.ds(me, 1)] = end_out[...][None]

    sides = wide // LANES
    parts = PEERS // sides
    rows = width // parts

    def values(g):
        if g + 1 < GROUPS:
            loads[7 + g].wait()
            pack((g + 1) * (wide // 128), (g + 2) * (wide // 128))
        at = pl.ds(g * wide, wide)
        row, lane = iota((128, wide), 0), iota((128, wide), 1)
        pick = (row % heads == g * (wide // hd) + lane // hd) & (row < 3 * heads)
        pick = pick.astype(F32).astype(BF16)
        held[g] = dot(dec[...], pick), dot(normed[...], w_val[:, at])

    def scale(g):
        at = pl.ds(g * wide, wide)
        cum, x = held.pop(g)
        grow_v[:, at] = jnp.exp2(cum)
        x_v[:, at] = x.astype(BF16)
        xs_v[:, at] = (x * jnp.exp2(-cum)).astype(BF16)
        state = (dot(b_t[...], xs_v[:, at]) * grow_v[count - 1 : count, at]).astype(BF16)
        for side in range(sides):
            s_out[g, pl.ds(side * parts, parts)] = state[
                :, side * LANES : (side + 1) * LANES
            ].reshape(parts, rows, LANES)
        for d in range(1, PEERS):
            slice_copy(s_out, s_in, send1, recv1, g, d).start()

    def gates(g):
        held[g] = dot(normed[...], w_gate[:, pl.ds(g * wide, wide)]).astype(BF16).astype(F32)

    def swish(g):
        z = held.pop(g)
        z = z * jax.nn.sigmoid(z)
        for k in range(wide // 128):
            sz_v[:, pl.ds(g * wide + 128 * k, 128)] = pltpu.roll(z[:, 128 * k : 128 * k + 128], hd, 1)

    def inner(g):
        at = pl.ds(g * wide, wide)
        for n in range(count // BIG):
            here = pl.ds(n * BIG, BIG)
            deep = (n + 1) * BIG
            sums = dot(masked[here, :deep], xs_v[:deep, at])
            y_v[here, at] = sums * grow_v[here, at] + skip_lanes[0:1, at] * x_v[here, at].astype(F32)

    def scan(g):
        first = (g * sides + me // parts) * (LANES // hd)
        pick = (iota((128, LANES), 0) == first + iota((128, LANES), 1) // hd).astype(F32)
        decay = exact(end_in[:, 0, :], pick)
        all_copies(s_out, s_in, send1, recv1, g).wait_recv()
        s_in[g, pl.ds(me, 1)] = s_out[g, pl.ds(me, 1)]
        running = jnp.zeros(s_in.shape[2:], F32)
        for k in range(PEERS):
            e_out[g, k] = running.astype(BF16)
            if k < PEERS - 1:
                running = decay[k : k + 1] * running + s_in[g, k].astype(F32)
        for d in range(1, PEERS):
            slice_copy(e_out, e_in, send2, recv2, g, d).start()
        e_in[g, pl.ds(me, 1)] = e_out[g, pl.ds(me, 1)]

    mean_of = jnp.where(
        iota((LANES, LANES), 0) // hd == iota((LANES, LANES), 1) // hd, 1.0 / hd, 0.0
    ).astype(BF16)

    def finish(g, n):
        here = pl.ds(n * ROWS, ROWS)
        for side in range(sides):
            at = pl.ds(g * wide + side * LANES, LANES)
            state = e_in[g, pl.ds(side * parts, parts)].reshape(width, LANES)
            y = y_v[here, at] + grow_v[here, at] * dot(c_rows[here, :], state)
            gated = y * sz_v[here, at]
            mean = dot((gated * gated).astype(BF16), mean_of)
            mixed[here, at] = (gated * lax.rsqrt(mean + 1e-05) * out_gain_ref[:, at]).astype(BF16)

    def store(n):
        here = pl.ds(n * ROWS, ROWS)
        return pltpu.make_async_copy(out_v.at[here], out_hbm.at[here], store_sem.at[n])

    def merge(g, n):
        here = pl.ds(n * ROWS, ROWS)
        at = pl.ds(g * wide, wide)
        part = dot(mixed[here, at], w_out[at, :])
        total = part + (encoded[here, :].astype(F32) if g == 0 else acc[here, :])
        if g < GROUPS - 1:
            acc[here, :] = total
        else:
            out_v[here, :] = total.astype(BF16)
            store(n).start()

    held = {}
    for g in range(GROUPS):
        values(g)
        scale(g)
    end_copy(1, PEERS - 1).wait_recv()
    spread = (iota((heads, lanes_all), 1) // hd == iota((heads, lanes_all), 0)).astype(F32)
    skip_lanes[...] = exact(jnp.broadcast_to(skip_ref[...], (8, heads)), spread)
    def mask(n):
        here, deep = pl.ds(n * BIG, BIG), (n + 1) * BIG
        causal = iota((BIG, deep), 0) + n * BIG >= iota((BIG, deep), 1)
        masked[here, :deep] = jnp.where(causal, dot(c_rows[here, :], b_t[:, :deep]), 0.0).astype(BF16)

    gates(0)
    gates(1)
    swish(0)
    swish(1)
    scan(0)
    gates(2)
    for n in range(count // BIG):
        mask(n)
    swish(2)
    scan(1)
    gates(3)
    inner(0)
    swish(3)
    scan(2)
    inner(1)
    inner(2)
    inner(3)
    scan(3)
    loads[6 + GROUPS].wait()
    for g in range(GROUPS):
        all_copies(e_out, e_in, send2, recv2, g).wait_recv()
        pipelined(functools.partial(finish, g), functools.partial(merge, g), blocks)

    end_copy(1, PEERS - 1).wait_send()
    for g in range(GROUPS):
        all_copies(s_out, s_in, send1, recv1, g).wait_send()
        all_copies(e_out, e_in, send2, recv2, g).wait_send()

    for n in range(blocks):
        store(n).wait()


def body(frames, patch_cell, enc_in, enc_bias, enc_out, pos_table, norm_gain, w_pair, w_keys,
         w_step, step_bias, decay_code, skip_gain, out_gain, w_out):
    count, pixels = frames.shape[0], frames.shape[2]
    depth = enc_out.shape[1]
    heads = w_step.shape[1]
    lanes = w_out.shape[0]
    width = w_keys.shape[1] // 2
    slice_rows = width * lanes // (GROUPS * PEERS * LANES)
    vm = pltpu.VMEM
    comm = vm((GROUPS, PEERS, slice_rows, LANES), BF16)
    dma = pltpu.SemaphoreType.DMA
    out = pl.pallas_call(
        kernel,
        out_shape=jax.ShapeDtypeStruct((count, depth), BF16),
        in_specs=[pl.BlockSpec(memory_space=pltpu.HBM)] * 8
        + [pl.BlockSpec(memory_space=pltpu.SMEM)]
        + [pl.BlockSpec(memory_space=pltpu.VMEM)] * 6,
        out_specs=pl.BlockSpec(memory_space=pl.ANY),
        scratch_shapes=[
            vm((count, pixels), BF16), vm((pixels, depth), BF16), vm((depth, depth), BF16),
            vm((pos_table.shape[0] // 16, 16, depth), BF16), vm((depth, 2 * width), BF16), vm((heads, depth), BF16),
            vm((depth, 2 * lanes), BF16), vm((lanes, depth), BF16),
            vm((count, depth), BF16), vm((count, depth), BF16),
            vm((count, depth), BF16), vm((depth, 128), BF16), vm((count, 128), BF16), vm((width, count), BF16),
            vm((count, width), BF16), vm((count, 128), BF16), vm((count, count), BF16),
            vm((depth, lanes), BF16), vm((depth, lanes), BF16), vm((count, lanes), BF16),
            vm((count, lanes), BF16),
            vm((count, lanes), F32), vm((count, lanes), F32), vm((count, lanes), F32),
            vm((count, depth), F32), vm((count, lanes), BF16), vm((8, lanes), F32),
            vm((count, depth), BF16), vm((8, 128), F32), vm((PEERS, 8, 128), F32), comm, comm, comm, comm,
            dma((7 + GROUPS,)), dma((count // ROWS,)), dma, dma,
            dma((GROUPS,)), dma((GROUPS,)), dma((GROUPS,)), dma((GROUPS,)),
        ],
        compiler_params=pltpu.CompilerParams(
            collective_id=0, has_side_effects=True, vmem_limit_bytes=VMEM_LIMIT
        ),
        name="layer",
    )(
        frames.reshape(count, pixels), enc_in, enc_out,
        pos_table.reshape(pos_table.shape[0] // 16, 16, depth), w_keys, w_step.T, w_pair, w_out,
        patch_cell, enc_bias[None], norm_gain[None], step_bias[None], decay_code[None],
        skip_gain[None], out_gain[None],
    )
    return out[:, None]


def solution(mesh):
    placed = (P("tm", "space", None), P("space")) + (P(),) * 13
    return jax.shard_map(
        body, mesh=mesh, in_specs=placed, out_specs=P("tm", "space", None), check_vma=False
    )
```

```python
import functools

import jax
import jax.numpy as jnp
from jax import lax
from jax.experimental import pallas as pl
from jax.experimental.pallas import tpu as pltpu
from jax.sharding import PartitionSpec as P

F32 = jnp.float32
BF16 = jnp.bfloat16
MESH = pl.DeviceIdType.MESH
GROUPS = 4
LANES = 256
PEERS = 16
SIDE = 4


def hops(step):
    return sum(min(d, SIDE - d) for d in step)


ROUTES = sorted(((n // SIDE, n % SIDE) for n in range(1, PEERS)), key=lambda s: (-hops(s), s))
ROWS = 256
BIG = 256
VMEM_LIMIT = 54 * 1024 * 1024


def dot(a, b):
    return jnp.dot(a, b, preferred_element_type=F32)


def exact(a, b):
    return jnp.dot(a, b, preferred_element_type=F32, precision=lax.Precision.HIGHEST)


def iota(shape, axis):
    return lax.broadcasted_iota(jnp.int32, shape, axis)


def pipelined(first, second, blocks, third=None):
    first(0)
    for n in range(blocks):
        if n + 1 < blocks:
            first(n + 1)
        second(n)
        if third is not None and n > 0:
            third(n - 1)
    if third is not None:
        third(blocks - 1)


def kernel(
    frames_hbm, enc_in_hbm, enc_out_hbm, pos_hbm, w_keys_hbm, w_step_hbm, w_pair_hbm, w_out_hbm,
    cell_ref, enc_bias_ref, norm_gain_ref, step_bias_ref, code_ref, skip_ref, out_gain_ref,
    out_hbm,
    frames, enc_in, enc_out, pos_table, w_keys, w_step, w_pair, w_out,
    hidden, encoded, normed, step_w, step_v, b_t, c_rows, dec, masked,
    w_val, w_gate, x_v, xs_v, sz_v, grow_v, y_v, acc, mixed, skip_lanes,
    out_v, end_out, end_in, s_out, s_in, e_out, e_in,
    load_sem, store_sem, end_send, end_recv, send1, recv1, send2, recv2,
):
    count, depth = encoded.shape
    heads = step_bias_ref.shape[1]
    width = c_rows.shape[1]
    lanes_all = x_v.shape[1]
    wide = lanes_all // GROUPS
    hd = lanes_all // heads
    me = lax.axis_index("tm")

    def pair_part(g):
        part = pl.ds(g * 2 * wide, 2 * wide)
        return (w_pair_hbm.at[:, part], w_pair.at[:, part])

    plan = [
        (frames_hbm, frames), (enc_in_hbm, enc_in), (enc_out_hbm, enc_out), (pos_hbm, pos_table),
        (w_keys_hbm, w_keys), (w_step_hbm, w_step),
    ]
    plan += [pair_part(g) for g in range(GROUPS)]
    plan.append((w_out_hbm, w_out))
    loads = [
        pltpu.make_async_copy(src, dst, load_sem.at[n]) for n, (src, dst) in enumerate(plan)
    ]
    for load in loads:
        load.start()

    barrier = pltpu.get_barrier_semaphore()

    def peer_at(d):
        dx, dy = ROUTES[d - 1]
        return lax.rem(lax.div(me, SIDE) + dx, SIDE) * SIDE + lax.rem(lax.rem(me, SIDE) + dy, SIDE)

    for d in range(1, PEERS):
        pl.semaphore_signal(barrier, inc=1, device_id={"tm": peer_at(d)}, device_id_type=MESH)

    four = (iota((heads, 128), 1) % heads == iota((heads, 128), 0)).astype(F32)
    bias4 = exact(jnp.broadcast_to(step_bias_ref[...], (8, heads)), four)[:1]
    code4 = dot(jnp.broadcast_to(code_ref[...], (8, heads)).astype(BF16), four.astype(BF16))[:1]
    rate4 = (-0.0005 - 0.003 * code4) * 1.4426950408889634
    loads[0].wait()
    loads[1].wait()

    def hide(n):
        at = pl.ds(n * BIG, BIG)
        raw = dot(frames[at, :], enc_in[...]) + enc_bias_ref[...]
        near = 0.5 * raw
        bent = jnp.tanh(raw * (0.7978845608028654 + 0.035677408136300125 * (raw * raw)))
        hidden[at, :] = (near + near * bent).astype(BF16)

    def draw(n):
        at = pl.ds(n * BIG, BIG)
        acc[at, :] = dot(hidden[at, :], enc_out[...])

    hide(0)
    loads[2].wait()
    pipelined(lambda n: hide(n) if n else None, draw, count // BIG)

    for n in (3, 4, 5, 6):
        loads[n].wait()
    cell = cell_ref[0]
    near = pos_table[lax.div(cell, 16)].astype(F32)
    pos_row = jnp.sum(
        jnp.where(iota((16, depth), 0) == lax.rem(cell, 16), near, 0.0), axis=0, keepdims=True
    )
    step_w[...] = jnp.concatenate([w_step[...]] * (128 // heads), axis=0).T

    def pack(first, last):
        for k in range(first, last):
            v0 = w_pair[:, 256 * k : 256 * k + 128]
            v1 = pltpu.roll(w_pair[:, 256 * k + 128 : 256 * k + 256], hd, 1)
            left = iota((depth, 128), 1) < hd
            w_val[:, 128 * k : 128 * k + 128] = jnp.where(left, v0, v1)
            w_gate[:, 128 * k : 128 * k + 128] = jnp.where(left, v1, v0)

    def code(n):
        at = pl.ds(n * ROWS, ROWS)
        coded = (acc[at, :] + pos_row).astype(BF16)
        encoded[at, :] = coded
        plain = coded.astype(F32)
        mean = jnp.mean(plain * plain, axis=-1, keepdims=True)
        normed[at, :] = (plain * lax.rsqrt(mean + 1e-05) * norm_gain_ref[...]).astype(BF16)

    def key(n):
        at = pl.ds(n * BIG, BIG)
        keys = dot(normed[at, :], w_keys[...]).astype(BF16)
        b_t[:, at] = keys[:, :width].T
        c_rows[at, :] = keys[:, width:]
        step_v[at, :] = jax.nn.sigmoid(dot(normed[at, :], step_w[...]) + bias4).astype(BF16)

    blocks = count // ROWS
    each = BIG // ROWS
    pack(0, wide // 128)
    pipelined(lambda n: [code(n * each + k) for k in range(each)], key, count // BIG)

    half = count // 2
    lane = iota((half, 128), 1)
    for top, deep in ((0, half), (half, count)):
        causal = iota((half, deep), 0) + top >= iota((half, deep), 1)
        cum = dot(causal.astype(F32).astype(BF16), step_v[:deep, :]) * rate4
        high = cum.astype(BF16).astype(F32)
        mid = (cum - high).astype(BF16).astype(F32)
        low = cum - high - mid
        part = lane // heads
        dec[top : top + half, :] = jnp.where(
            part == 0, high, jnp.where(part == 1, mid, jnp.where(part == 2, low, 0.0))
        ).astype(BF16)
    end_out[...] = jnp.broadcast_to(jnp.exp2(cum[half - 1 : half]), (8, 128))

    pl.semaphore_wait(barrier, PEERS - 1)

    def end_copy(d, n=None):
        return pltpu.make_async_remote_copy(
            src_ref=end_out if n is None else end_in.at[pl.ds(0, n)],
            dst_ref=end_in.at[me] if n is None else end_in.at[pl.ds(0, n)],
            send_sem=end_send, recv_sem=end_recv, device_id={"tm": peer_at(d)}, device_id_type=MESH,
        )

    def slice_copy(src, dst, send, recv, g, d):
        return pltpu.make_async_remote_copy(
            src_ref=src.at[g, peer_at(d)], dst_ref=dst.at[g, me], send_sem=send.at[g],
            recv_sem=recv.at[g], device_id={"tm": peer_at(d)}, device_id_type=MESH,
        )

    def all_copies(src, dst, send, recv, g):
        every = pl.ds(0, PEERS - 1)
        return pltpu.make_async_remote_copy(
            src_ref=src.at[g, every], dst_ref=dst.at[g, every], send_sem=send.at[g],
            recv_sem=recv.at[g], device_id={"tm": peer_at(1)}, device_id_type=MESH,
        )

    for d in range(1, PEERS):
        end_copy(d).start()
    end_in[pl.ds(me, 1)] = end_out[...][None]

    sides = wide // LANES
    parts = PEERS // sides
    rows = width // parts

    def values(g):
        if g + 1 < GROUPS:
            loads[7 + g].wait()
            pack((g + 1) * (wide // 128), (g + 2) * (wide // 128))
        at = pl.ds(g * wide, wide)
        row, lane = iota((128, wide), 0), iota((128, wide), 1)
        pick = (row % heads == g * (wide // hd) + lane // hd) & (row < 3 * heads)
        pick = pick.astype(F32).astype(BF16)
        held[g] = dot(dec[...], pick), dot(normed[...], w_val[:, at])

    def scale(g):
        at = pl.ds(g * wide, wide)
        cum, x = held.pop(g)
        grow_v[:, at] = jnp.exp2(cum)
        x_v[:, at] = x.astype(BF16)
        xs_v[:, at] = (x * jnp.exp2(-cum)).astype(BF16)
        state = (dot(b_t[...], xs_v[:, at]) * grow_v[count - 1 : count, at]).astype(BF16)
        for side in range(sides):
            s_out[g, pl.ds(side * parts, parts)] = state[
                :, side * LANES : (side + 1) * LANES
            ].reshape(parts, rows, LANES)
        for d in range(1, PEERS):
            slice_copy(s_out, s_in, send1, recv1, g, d).start()

    def gates(g):
        held[g] = dot(normed[...], w_gate[:, pl.ds(g * wide, wide)]).astype(BF16).astype(F32)

    def swish(g):
        z = held.pop(g)
        z = z * jax.nn.sigmoid(z)
        for k in range(wide // 128):
            sz_v[:, pl.ds(g * wide + 128 * k, 128)] = pltpu.roll(z[:, 128 * k : 128 * k + 128], hd, 1)

    def inner(g):
        at = pl.ds(g * wide, wide)
        for n in range(count // BIG):
            here = pl.ds(n * BIG, BIG)
            deep = (n + 1) * BIG
            sums = dot(masked[here, :deep], xs_v[:deep, at])
            y_v[here, at] = sums * grow_v[here, at] + skip_lanes[0:1, at] * x_v[here, at].astype(F32)

    def scan(g):
        first = (g * sides + me // parts) * (LANES // hd)
        pick = (iota((128, LANES), 0) == first + iota((128, LANES), 1) // hd).astype(F32)
        decay = exact(end_in[:, 0, :], pick)
        all_copies(s_out, s_in, send1, recv1, g).wait_recv()
        s_in[g, pl.ds(me, 1)] = s_out[g, pl.ds(me, 1)]
        running = jnp.zeros(s_in.shape[2:], F32)
        for k in range(PEERS):
            e_out[g, k] = running.astype(BF16)
            if k < PEERS - 1:
                running = decay[k : k + 1] * running + s_in[g, k].astype(F32)
        for d in range(1, PEERS):
            slice_copy(e_out, e_in, send2, recv2, g, d).start()
        e_in[g, pl.ds(me, 1)] = e_out[g, pl.ds(me, 1)]

    mean_of = jnp.where(
        iota((LANES, LANES), 0) // hd == iota((LANES, LANES), 1) // hd, 1.0 / hd, 0.0
    ).astype(BF16)

    def finish(g, n):
        here = pl.ds(n * ROWS, ROWS)
        for side in range(sides):
            at = pl.ds(g * wide + side * LANES, LANES)
            state = e_in[g, pl.ds(side * parts, parts)].reshape(width, LANES)
            y = y_v[here, at] + grow_v[here, at] * dot(c_rows[here, :], state)
            gated = y * sz_v[here, at]
            mean = dot((gated * gated).astype(BF16), mean_of)
            mixed[here, at] = (gated * lax.rsqrt(mean + 1e-05) * out_gain_ref[:, at]).astype(BF16)

    def store(n):
        here = pl.ds(n * ROWS, ROWS)
        return pltpu.make_async_copy(out_v.at[here], out_hbm.at[here], store_sem.at[n])

    def merge(g, n):
        here = pl.ds(n * ROWS, ROWS)
        at = pl.ds(g * wide, wide)
        part = dot(mixed[here, at], w_out[at, :])
        total = part + (encoded[here, :].astype(F32) if g == 0 else acc[here, :])
        if g < GROUPS - 1:
            acc[here, :] = total
        else:
            out_v[here, :] = total.astype(BF16)
            store(n).start()

    held = {}
    for g in range(GROUPS):
        values(g)
        scale(g)
    end_copy(1, PEERS - 1).wait_recv()
    spread = (iota((heads, lanes_all), 1) // hd == iota((heads, lanes_all), 0)).astype(F32)
    skip_lanes[...] = exact(jnp.broadcast_to(skip_ref[...], (8, heads)), spread)
    def mask(n):
        here, deep = pl.ds(n * BIG, BIG), (n + 1) * BIG
        causal = iota((BIG, deep), 0) + n * BIG >= iota((BIG, deep), 1)
        masked[here, :deep] = jnp.where(causal, dot(c_rows[here, :], b_t[:, :deep]), 0.0).astype(BF16)

    gates(0)
    gates(1)
    swish(0)
    swish(1)
    scan(0)
    gates(2)
    for n in range(count // BIG):
        mask(n)
    swish(2)
    scan(1)
    gates(3)
    inner(0)
    swish(3)
    scan(2)
    inner(1)
    inner(2)
    inner(3)
    scan(3)
    loads[6 + GROUPS].wait()
    for g in range(GROUPS):
        all_copies(e_out, e_in, send2, recv2, g).wait_recv()
        pipelined(functools.partial(finish, g), functools.partial(merge, g), blocks)

    end_copy(1, PEERS - 1).wait_send()
    for g in range(GROUPS):
        all_copies(s_out, s_in, send1, recv1, g).wait_send()
        all_copies(e_out, e_in, send2, recv2, g).wait_send()

    for n in range(blocks):
        store(n).wait()


def body(frames, patch_cell, enc_in, enc_bias, enc_out, pos_table, norm_gain, w_pair, w_keys,
         w_step, step_bias, decay_code, skip_gain, out_gain, w_out):
    count, pixels = frames.shape[0], frames.shape[2]
    depth = enc_out.shape[1]
    heads = w_step.shape[1]
    lanes = w_out.shape[0]
    width = w_keys.shape[1] // 2
    slice_rows = width * lanes // (GROUPS * PEERS * LANES)
    vm = pltpu.VMEM
    comm = vm((GROUPS, PEERS, slice_rows, LANES), BF16)
    dma = pltpu.SemaphoreType.DMA
    out = pl.pallas_call(
        kernel,
        out_shape=jax.ShapeDtypeStruct((count, depth), BF16),
        in_specs=[pl.BlockSpec(memory_space=pltpu.HBM)] * 8
        + [pl.BlockSpec(memory_space=pltpu.SMEM)]
        + [pl.BlockSpec(memory_space=pltpu.VMEM)] * 6,
        out_specs=pl.BlockSpec(memory_space=pl.ANY),
        scratch_shapes=[
            vm((count, pixels), BF16), vm((pixels, depth), BF16), vm((depth, depth), BF16),
            vm((pos_table.shape[0] // 16, 16, depth), BF16), vm((depth, 2 * width), BF16), vm((heads, depth), BF16),
            vm((depth, 2 * lanes), BF16), vm((lanes, depth), BF16),
            vm((count, depth), BF16), vm((count, depth), BF16),
            vm((count, depth), BF16), vm((depth, 128), BF16), vm((count, 128), BF16), vm((width, count), BF16),
            vm((count, width), BF16), vm((count, 128), BF16), vm((count, count), BF16),
            vm((depth, lanes), BF16), vm((depth, lanes), BF16), vm((count, lanes), BF16),
            vm((count, lanes), BF16),
            vm((count, lanes), F32), vm((count, lanes), F32), vm((count, lanes), F32),
            vm((count, depth), F32), vm((count, lanes), BF16), vm((8, lanes), F32),
            vm((count, depth), BF16), vm((8, 128), F32), vm((PEERS, 8, 128), F32), comm, comm, comm, comm,
            dma((7 + GROUPS,)), dma((count // ROWS,)), dma, dma,
            dma((GROUPS,)), dma((GROUPS,)), dma((GROUPS,)), dma((GROUPS,)),
        ],
        compiler_params=pltpu.CompilerParams(
            collective_id=0, has_side_effects=True, vmem_limit_bytes=VMEM_LIMIT
        ),
        name="layer",
    )(
        frames.reshape(count, pixels), enc_in, enc_out,
        pos_table.reshape(pos_table.shape[0] // 16, 16, depth), w_keys, w_step.T, w_pair, w_out,
        patch_cell, enc_bias[None], norm_gain[None], step_bias[None], decay_code[None],
        skip_gain[None], out_gain[None],
    )
    return out[:, None]


def solution(mesh):
    placed = (P("tm", "space", None), P("space")) + (P(),) * 13
    return jax.shard_map(
        body, mesh=mesh, in_specs=placed, out_specs=P("tm", "space", None), check_vma=False
    )
```

```python
import functools

import jax
import jax.numpy as jnp
from jax import lax
from jax.experimental import pallas as pl
from jax.experimental.pallas import tpu as pltpu
from jax.sharding import PartitionSpec as P

F32 = jnp.float32
BF16 = jnp.bfloat16
MESH = pl.DeviceIdType.MESH
GROUPS = 4
LANES = 256
PEERS = 16
SIDE = 4


def hops(step):
    return sum(min(d, SIDE - d) for d in step)


ROUTES = sorted(((n // SIDE, n % SIDE) for n in range(1, PEERS)), key=lambda s: (-hops(s), s))
ROWS = 256
BIG = 256
VMEM_LIMIT = 54 * 1024 * 1024


def dot(a, b):
    return jnp.dot(a, b, preferred_element_type=F32)


def exact(a, b):
    return jnp.dot(a, b, preferred_element_type=F32, precision=lax.Precision.HIGHEST)


def iota(shape, axis):
    return lax.broadcasted_iota(jnp.int32, shape, axis)


def pipelined(first, second, blocks, third=None):
    first(0)
    for n in range(blocks):
        if n + 1 < blocks:
            first(n + 1)
        second(n)
        if third is not None and n > 0:
            third(n - 1)
    if third is not None:
        third(blocks - 1)


def kernel(
    frames_hbm, enc_in_hbm, enc_out_hbm, pos_hbm, w_keys_hbm, w_step_hbm, w_pair_hbm, w_out_hbm,
    cell_ref, enc_bias_ref, norm_gain_ref, step_bias_ref, code_ref, skip_ref, out_gain_ref,
    out_hbm,
    frames, enc_in, enc_out, pos_table, w_keys, w_step, w_pair, w_out,
    hidden, encoded, normed, step_w, step_v, b_t, c_rows, dec, masked,
    w_val, w_gate, x_v, xs_v, sz_v, grow_v, y_v, acc, mixed, skip_lanes,
    out_v, end_out, end_in, s_out, s_in, e_out, e_in,
    load_sem, store_sem, end_send, end_recv, send1, recv1, send2, recv2,
):
    count, depth = encoded.shape
    heads = step_bias_ref.shape[1]
    width = c_rows.shape[1]
    lanes_all = x_v.shape[1]
    wide = lanes_all // GROUPS
    hd = lanes_all // heads
    me = lax.axis_index("tm")

    def pair_part(g):
        part = pl.ds(g * 2 * wide, 2 * wide)
        return (w_pair_hbm.at[:, part], w_pair.at[:, part])

    plan = [
        (frames_hbm, frames), (enc_in_hbm, enc_in), (enc_out_hbm, enc_out), (pos_hbm, pos_table),
        (w_keys_hbm, w_keys), (w_step_hbm, w_step),
    ]
    plan += [pair_part(g) for g in range(GROUPS)]
    plan.append((w_out_hbm, w_out))
    loads = [
        pltpu.make_async_copy(src, dst, load_sem.at[n]) for n, (src, dst) in enumerate(plan)
    ]
    for load in loads:
        load.start()

    barrier = pltpu.get_barrier_semaphore()

    def peer_at(d):
        dx, dy = ROUTES[d - 1]
        return lax.rem(lax.div(me, SIDE) + dx, SIDE) * SIDE + lax.rem(lax.rem(me, SIDE) + dy, SIDE)

    for d in range(1, PEERS):
        pl.semaphore_signal(barrier, inc=1, device_id={"tm": peer_at(d)}, device_id_type=MESH)

    four = (iota((heads, 128), 1) % heads == iota((heads, 128), 0)).astype(F32)
    bias4 = exact(jnp.broadcast_to(step_bias_ref[...], (8, heads)), four)[:1]
    code4 = dot(jnp.broadcast_to(code_ref[...], (8, heads)).astype(BF16), four.astype(BF16))[:1]
    rate4 = (-0.0005 - 0.003 * code4) * 1.4426950408889634
    spread = (iota((heads, lanes_all), 1) // hd == iota((heads, lanes_all), 0)).astype(F32)
    skip_lanes[...] = exact(jnp.broadcast_to(skip_ref[...], (8, heads)), spread)
    loads[0].wait()
    loads[1].wait()

    def hide(n):
        at = pl.ds(n * BIG, BIG)
        raw = dot(frames[at, :], enc_in[...]) + enc_bias_ref[...]
        near = 0.5 * raw
        bent = jnp.tanh(raw * (0.7978845608028654 + 0.035677408136300125 * (raw * raw)))
        hidden[at, :] = (near + near * bent).astype(BF16)

    def draw(n):
        at = pl.ds(n * BIG, BIG)
        acc[at, :] = dot(hidden[at, :], enc_out[...])

    hide(0)
    loads[2].wait()
    pipelined(lambda n: hide(n) if n else None, draw, count // BIG)

    for n in (3, 4, 5, 6):
        loads[n].wait()
    cell = cell_ref[0]
    near = pos_table[lax.div(cell, 16)].astype(F32)
    pos_row = jnp.sum(
        jnp.where(iota((16, depth), 0) == lax.rem(cell, 16), near, 0.0), axis=0, keepdims=True
    )
    step_w[...] = jnp.concatenate([w_step[...]] * (128 // heads), axis=0).T

    def pack(first, last):
        for k in range(first, last):
            v0 = w_pair[:, 256 * k : 256 * k + 128]
            v1 = pltpu.roll(w_pair[:, 256 * k + 128 : 256 * k + 256], hd, 1)
            left = iota((depth, 128), 1) < hd
            w_val[:, 128 * k : 128 * k + 128] = jnp.where(left, v0, v1)
            w_gate[:, 128 * k : 128 * k + 128] = jnp.where(left, v1, v0)

    def code(n):
        at = pl.ds(n * ROWS, ROWS)
        coded = (acc[at, :] + pos_row).astype(BF16)
        encoded[at, :] = coded
        plain = coded.astype(F32)
        mean = jnp.mean(plain * plain, axis=-1, keepdims=True)
        normed[at, :] = (plain * lax.rsqrt(mean + 1e-05) * norm_gain_ref[...]).astype(BF16)

    def key(n):
        at = pl.ds(n * BIG, BIG)
        keys = dot(normed[at, :], w_keys[...]).astype(BF16)
        b_t[:, at] = keys[:, :width].T
        c_rows[at, :] = keys[:, width:]
        step_v[at, :] = jax.nn.sigmoid(dot(normed[at, :], step_w[...]) + bias4).astype(BF16)

    blocks = count // ROWS
    each = BIG // ROWS
    pack(0, wide // 128)
    pipelined(lambda n: [code(n * each + k) for k in range(each)], key, count // BIG)

    half = count // 2
    lane = iota((half, 128), 1)
    for top, deep in ((0, half), (half, count)):
        causal = iota((half, deep), 0) + top >= iota((half, deep), 1)
        cum = dot(causal.astype(F32).astype(BF16), step_v[:deep, :]) * rate4
        high = cum.astype(BF16).astype(F32)
        mid = (cum - high).astype(BF16).astype(F32)
        low = cum - high - mid
        part = lane // heads
        dec[top : top + half, :] = jnp.where(
            part == 0, high, jnp.where(part == 1, mid, jnp.where(part == 2, low, 0.0))
        ).astype(BF16)
    end_out[...] = jnp.broadcast_to(jnp.exp2(cum[half - 1 : half]), (8, 128))

    pl.semaphore_wait(barrier, PEERS - 1)

    def end_copy(d, n=None):
        return pltpu.make_async_remote_copy(
            src_ref=end_out if n is None else end_in.at[pl.ds(0, n)],
            dst_ref=end_in.at[me] if n is None else end_in.at[pl.ds(0, n)],
            send_sem=end_send, recv_sem=end_recv, device_id={"tm": peer_at(d)}, device_id_type=MESH,
        )

    def slice_copy(src, dst, send, recv, g, d):
        return pltpu.make_async_remote_copy(
            src_ref=src.at[g, peer_at(d)], dst_ref=dst.at[g, me], send_sem=send.at[g],
            recv_sem=recv.at[g], device_id={"tm": peer_at(d)}, device_id_type=MESH,
        )

    def all_copies(src, dst, send, recv, g):
        every = pl.ds(0, PEERS - 1)
        return pltpu.make_async_remote_copy(
            src_ref=src.at[g, every], dst_ref=dst.at[g, every], send_sem=send.at[g],
            recv_sem=recv.at[g], device_id={"tm": peer_at(1)}, device_id_type=MESH,
        )

    for d in range(1, PEERS):
        end_copy(d).start()
    end_in[pl.ds(me, 1)] = end_out[...][None]

    sides = wide // LANES
    parts = PEERS // sides
    rows = width // parts

    def values(g):
        if g + 1 < GROUPS:
            loads[7 + g].wait()
            pack((g + 1) * (wide // 128), (g + 2) * (wide // 128))
        at = pl.ds(g * wide, wide)
        row, lane = iota((128, wide), 0), iota((128, wide), 1)
        pick = (row % heads == g * (wide // hd) + lane // hd) & (row < 3 * heads)
        pick = pick.astype(F32).astype(BF16)
        held[g] = dot(dec[...], pick), dot(normed[...], w_val[:, at])

    def scale(g):
        at = pl.ds(g * wide, wide)
        cum, x = held.pop(g)
        grow_v[:, at] = jnp.exp2(cum)
        x_v[:, at] = x.astype(BF16)
        xs_v[:, at] = (x * jnp.exp2(-cum)).astype(BF16)
        state = (dot(b_t[...], xs_v[:, at]) * grow_v[count - 1 : count, at]).astype(BF16)
        for side in range(sides):
            s_out[g, pl.ds(side * parts, parts)] = state[
                :, side * LANES : (side + 1) * LANES
            ].reshape(parts, rows, LANES)
        for d in range(1, PEERS):
            slice_copy(s_out, s_in, send1, recv1, g, d).start()

    def gates(g):
        held[g] = dot(normed[...], w_gate[:, pl.ds(g * wide, wide)]).astype(BF16).astype(F32)

    def swish(g):
        z = held.pop(g)
        z = z * jax.nn.sigmoid(z)
        for k in range(wide // 128):
            sz_v[:, pl.ds(g * wide + 128 * k, 128)] = pltpu.roll(z[:, 128 * k : 128 * k + 128], hd, 1)

    def inner(g):
        at = pl.ds(g * wide, wide)
        for n in range(count // BIG):
            here = pl.ds(n * BIG, BIG)
            deep = (n + 1) * BIG
            sums = dot(masked[here, :deep], xs_v[:deep, at])
            y_v[here, at] = sums * grow_v[here, at] + skip_lanes[0:1, at] * x_v[here, at].astype(F32)

    def scan(g):
        first = (g * sides + me // parts) * (LANES // hd)
        pick = (iota((128, LANES), 0) == first + iota((128, LANES), 1) // hd).astype(F32)
        decay = exact(end_in[:, 0, :], pick)
        all_copies(s_out, s_in, send1, recv1, g).wait_recv()
        s_in[g, pl.ds(me, 1)] = s_out[g, pl.ds(me, 1)]
        running = jnp.zeros(s_in.shape[2:], F32)
        for k in range(PEERS):
            e_out[g, k] = running.astype(BF16)
            if k < PEERS - 1:
                running = decay[k : k + 1] * running + s_in[g, k].astype(F32)
        for d in range(1, PEERS):
            slice_copy(e_out, e_in, send2, recv2, g, d).start()
        e_in[g, pl.ds(me, 1)] = e_out[g, pl.ds(me, 1)]

    mean_of = jnp.where(
        iota((LANES, LANES), 0) // hd == iota((LANES, LANES), 1) // hd, 1.0 / hd, 0.0
    ).astype(BF16)

    def finish(g, n):
        here = pl.ds(n * ROWS, ROWS)
        for side in range(sides):
            at = pl.ds(g * wide + side * LANES, LANES)
            state = e_in[g, pl.ds(side * parts, parts)].reshape(width, LANES)
            y = y_v[here, at] + grow_v[here, at] * dot(c_rows[here, :], state)
            gated = y * sz_v[here, at]
            mean = dot((gated * gated).astype(BF16), mean_of)
            mixed[here, at] = (gated * lax.rsqrt(mean + 1e-05) * out_gain_ref[:, at]).astype(BF16)

    def store(n):
        here = pl.ds(n * ROWS, ROWS)
        return pltpu.make_async_copy(out_v.at[here], out_hbm.at[here], store_sem.at[n])

    def merge(g, n):
        here = pl.ds(n * ROWS, ROWS)
        at = pl.ds(g * wide, wide)
        part = dot(mixed[here, at], w_out[at, :])
        total = part + (encoded[here, :].astype(F32) if g == 0 else acc[here, :])
        if g < GROUPS - 1:
            acc[here, :] = total
        else:
            out_v[here, :] = total.astype(BF16)
            store(n).start()

    held = {}
    for g in range(GROUPS):
        values(g)
        scale(g)
    end_copy(1, PEERS - 1).wait_recv()
    def mask(n):
        here, deep = pl.ds(n * BIG, BIG), (n + 1) * BIG
        causal = iota((BIG, deep), 0) + n * BIG >= iota((BIG, deep), 1)
        masked[here, :deep] = jnp.where(causal, dot(c_rows[here, :], b_t[:, :deep]), 0.0).astype(BF16)

    gates(0)
    gates(1)
    swish(0)
    swish(1)
    scan(0)
    gates(2)
    for n in range(count // BIG):
        mask(n)
    swish(2)
    scan(1)
    gates(3)
    inner(0)
    swish(3)
    scan(2)
    inner(1)
    inner(2)
    inner(3)
    scan(3)
    loads[6 + GROUPS].wait()
    for g in range(GROUPS):
        all_copies(e_out, e_in, send2, recv2, g).wait_recv()
        pipelined(functools.partial(finish, g), functools.partial(merge, g), blocks)

    end_copy(1, PEERS - 1).wait_send()
    for g in range(GROUPS):
        all_copies(s_out, s_in, send1, recv1, g).wait_send()
        all_copies(e_out, e_in, send2, recv2, g).wait_send()

    for n in range(blocks):
        store(n).wait()


def body(frames, patch_cell, enc_in, enc_bias, enc_out, pos_table, norm_gain, w_pair, w_keys,
         w_step, step_bias, decay_code, skip_gain, out_gain, w_out):
    count, pixels = frames.shape[0], frames.shape[2]
    depth = enc_out.shape[1]
    heads = w_step.shape[1]
    lanes = w_out.shape[0]
    width = w_keys.shape[1] // 2
    slice_rows = width * lanes // (GROUPS * PEERS * LANES)
    vm = pltpu.VMEM
    comm = vm((GROUPS, PEERS, slice_rows, LANES), BF16)
    dma = pltpu.SemaphoreType.DMA
    out = pl.pallas_call(
        kernel,
        out_shape=jax.ShapeDtypeStruct((count, depth), BF16),
        in_specs=[pl.BlockSpec(memory_space=pltpu.HBM)] * 8
        + [pl.BlockSpec(memory_space=pltpu.SMEM)]
        + [pl.BlockSpec(memory_space=pltpu.VMEM)] * 6,
        out_specs=pl.BlockSpec(memory_space=pl.ANY),
        scratch_shapes=[
            vm((count, pixels), BF16), vm((pixels, depth), BF16), vm((depth, depth), BF16),
            vm((pos_table.shape[0] // 16, 16, depth), BF16), vm((depth, 2 * width), BF16), vm((heads, depth), BF16),
            vm((depth, 2 * lanes), BF16), vm((lanes, depth), BF16),
            vm((count, depth), BF16), vm((count, depth), BF16),
            vm((count, depth), BF16), vm((depth, 128), BF16), vm((count, 128), BF16), vm((width, count), BF16),
            vm((count, width), BF16), vm((count, 128), BF16), vm((count, count), BF16),
            vm((depth, lanes), BF16), vm((depth, lanes), BF16), vm((count, lanes), BF16),
            vm((count, lanes), BF16),
            vm((count, lanes), F32), vm((count, lanes), F32), vm((count, lanes), F32),
            vm((count, depth), F32), vm((count, lanes), BF16), vm((8, lanes), F32),
            vm((count, depth), BF16), vm((8, 128), F32), vm((PEERS, 8, 128), F32), comm, comm, comm, comm,
            dma((7 + GROUPS,)), dma((count // ROWS,)), dma, dma,
            dma((GROUPS,)), dma((GROUPS,)), dma((GROUPS,)), dma((GROUPS,)),
        ],
        compiler_params=pltpu.CompilerParams(
            collective_id=0, has_side_effects=True, vmem_limit_bytes=VMEM_LIMIT
        ),
        name="layer",
    )(
        frames.reshape(count, pixels), enc_in, enc_out,
        pos_table.reshape(pos_table.shape[0] // 16, 16, depth), w_keys, w_step.T, w_pair, w_out,
        patch_cell, enc_bias[None], norm_gain[None], step_bias[None], decay_code[None],
        skip_gain[None], out_gain[None],
    )
    return out[:, None]


def solution(mesh):
    placed = (P("tm", "space", None), P("space")) + (P(),) * 13
    return jax.shard_map(
        body, mesh=mesh, in_specs=placed, out_specs=P("tm", "space", None), check_vma=False
    )
```
